32 devices in a mesh: seq: 8 (over z, y), head: 4 (over x, core).
Axes of the slice: x: 2, y: 2, z: 4, core: 2. Of those that a mesh axis runs over, the one named last changes fastest.
Arguments:
- queries: bfloat16 [8192, 512], P('seq', 'head'), may hold values from -6 to 6
- keys: bfloat16 [8192, 512], P('seq', 'head'), may hold values from -6 to 6
- values: bfloat16 [8192, 512], P('seq', 'head'), may hold values from -6 to 6
- out_grad: bfloat16 [8192, 512], P('seq', 'head'), may hold values from -6 to 6
- lengths: int32 [4], replicated, may hold values from 1 to 3072, 8192 in all
- w_proj: bfloat16 [3, 512, 512], P(None, None, 'head'), may hold values from -0.25 to 0.25
Outputs:
- d_input: float32 [8192, 512], P(('seq', 'head'))
The draws below stay inside these ranges and needn't reach their ends.
Inputs may be any that keep to these rules, and one draw needn't show every extreme that they name: The lengths sum to 8192; the longest is exactly 3072.
All inputs are finite; a program needn't handle non-finite values.
Results may differ from the reference program's by a relative error of at most 0.006.
Values may be sent and summed in bfloat16 or wider, within the bound.
No kernel may reach another device: no remote copies, remote signals or barrier semaphores. Data moves between devices by JAX's collectives and lax.ppermute only.
A program may use at most 64 MiB of HBM per device.

```python
import math
import jax
import jax.numpy as jnp
import numpy as np
from jax import lax

D = 512
HEAD = 128
ROWS = 1024
LAGS = 4
TOKENS = 8192
USERS = 4
MAXLEN = 3072


def shard_levels(key, dims, cuts, smallest, largest):
    level, own = 1.0, jax.random.fold_in(key, 6)
    for dim, blocks in cuts:
        draws = jnp.exp(jax.random.uniform(jax.random.fold_in(own, dim), (blocks,), jnp.float32, smallest / len(cuts), largest / len(cuts)))
        level = level * jnp.repeat(draws, dims[dim] // blocks).reshape([-1 if axis == dim else 1 for axis in range(len(dims))])
    return level


def profile(number_of, total, reach, slope):
    portions = [(1 << 20) // math.isqrt(standing ** slope) + 1 for standing in range(2, number_of + 1)]
    spare, holding = total - reach - (number_of - 1), [1] * (number_of - 1)
    while spare > 0:
        movable = [i for i in range(number_of - 1) if holding[i] < reach]
        pool, budget = sum([portions[i] for i in movable]), spare
        for i in movable:
            extra = min(reach - holding[i], max(1, budget * portions[i] // pool), spare)
            holding[i] = holding[i] + extra
            spare = spare - extra
    return np.array([reach] + holding)


def ragged(key, amount, total, limit, skew):
    if amount == 2:
        one = jax.random.randint(key, (), max(1, total - limit), min(limit, total - 1) + 1)
        return jnp.stack([one, total - one])
    sizes = jnp.asarray(profile(amount, total, limit, skew), jnp.int32)
    couples = (amount - 1) // 2
    donor, receiver = sizes[1:1 + 2 * couples:2], sizes[2:2 + 2 * couples:2]
    margin = jnp.minimum(donor - 1, limit - receiver)
    moved = jax.random.randint(jax.random.fold_in(key, 1), (couples,), 0, 1 << 20) % (margin + 1)
    sizes = sizes.at[1:1 + 2 * couples:2].set(donor - moved).at[2:2 + 2 * couples:2].set(receiver + moved)
    return sizes[jax.random.permutation(jax.random.fold_in(key, 2), amount)]


def bell_draw(rng, extent, scale, bound, pieces=(), held_as=jnp.bfloat16):
    entries = jax.random.normal(rng, extent, jnp.float32) * scale
    if len(pieces) > 0:
        entries = shard_levels(rng, extent, pieces, -0.22, 0.18) * entries
    return jnp.clip(entries, min=-bound, max=bound).astype(held_as)


def setup_inputs(seed: int = 0) -> dict:
    key_list = jax.random.split(jax.random.key(seed), 7)
    return {
        "queries": bell_draw(key_list[0], (TOKENS, D), 1.0, 6.0, ((0, 8), (1, 4))),
        "keys": bell_draw(key_list[1], (TOKENS, D), 1.0, 6.0, ((0, 8), (1, 4))),
        "values": bell_draw(key_list[2], (TOKENS, D), 1.0, 6.0, ((0, 8), (1, 4))),
        "out_grad": bell_draw(key_list[3], (TOKENS, D), 1.0, 6.0, ((0, 8), (1, 4))),
        "lengths": ragged(key_list[4], USERS, TOKENS, MAXLEN, 2).astype(jnp.int32),
        "w_proj": bell_draw(key_list[5], (3, D, D), D ** -0.5, 0.25, ((2, 4),)),
    }


def pair_task(query_tile, grad_tile, key_tile, value_tile, query_start, key_start, user_ends):
    tile_rows = query_tile.shape[0]
    score_scale = HEAD ** (-0.5)
    norm_factor = 1.0 / math.sqrt(MAXLEN)
    offsets = lax.iota(jnp.int32, tile_rows)
    query_pos = query_start + offsets
    key_pos = key_start + offsets
    query_user = lax.optimization_barrier(jnp.sum((user_ends[None, :] <= query_pos[:, None]).astype(jnp.int32), axis=1))
    key_user = lax.optimization_barrier(jnp.sum((user_ends[None, :] <= key_pos[:, None]).astype(jnp.int32), axis=1))
    visible = (key_pos[None, :] <= query_pos[:, None]) & (query_user[:, None] == key_user[None, :])
    visible = visible[None, :, :]
    query_wide = query_tile.astype(jnp.float32)
    grad_wide = grad_tile.astype(jnp.float32)
    key_wide = key_tile.astype(jnp.float32)
    value_wide = value_tile.astype(jnp.float32)
    highest = lax.Precision.HIGHEST
    scores = jnp.einsum('qnh,knh->nqk', query_wide, key_wide, precision=highest) * score_scale
    gate_prob = jax.nn.sigmoid(scores)
    weights = jnp.where(visible, scores * gate_prob * norm_factor, 0.0).astype(jnp.bfloat16)
    d_weights = jnp.einsum('qnh,knh->nqk', grad_wide, value_wide, precision=highest)
    d_scores = jnp.where(visible, d_weights * gate_prob * (1.0 + scores * (1.0 - gate_prob)) * norm_factor, 0.0).astype(jnp.bfloat16)
    d_scores_wide = d_scores.astype(jnp.float32)
    weights_wide = weights.astype(jnp.float32)
    query_grad = (jnp.einsum('nqk,knh->qnh', d_scores_wide, key_wide, precision=highest) * score_scale).astype(jnp.bfloat16)
    key_grad = (jnp.einsum('nqk,qnh->knh', d_scores_wide, query_wide, precision=highest) * score_scale).astype(jnp.bfloat16)
    value_grad = jnp.einsum('nqk,qnh->knh', weights_wide, grad_wide, precision=highest).astype(jnp.bfloat16)
    return (query_grad, jnp.stack([key_grad, value_grad]))

def reference(queries, keys, values, out_grad, lengths, w_proj):
    heads = D // HEAD
    tile_count = TOKENS // ROWS
    user_ends = jnp.cumsum(lengths).astype(jnp.int32)
    tiled = (tile_count, ROWS, heads, HEAD)
    query_tiles = queries.reshape(tiled)
    key_tiles = keys.reshape(tiled)
    value_tiles = values.reshape(tiled)
    grad_tiles = out_grad.reshape(tiled)

    def last_user(position):
        return jnp.sum((user_ends <= position).astype(jnp.int32))

    def per_tile(pair_acc, tile_index):
        query_start = tile_index * ROWS
        query_tile = lax.dynamic_index_in_dim(query_tiles, tile_index, 0, keepdims=False)
        grad_tile = lax.dynamic_index_in_dim(grad_tiles, tile_index, 0, keepdims=False)
        query_total = jnp.zeros((ROWS, heads, HEAD), jnp.float32)
        zero_parts = (jnp.zeros((ROWS, heads, HEAD), jnp.bfloat16), jnp.zeros((2, ROWS, heads, HEAD), jnp.bfloat16))
        for offset in range(LAGS):
            key_index = tile_index - offset
            safe_index = jnp.maximum(key_index, 0)
            key_start = key_index * ROWS
            if offset == 0:
                live = key_index >= 0
            else:
                live = (key_index >= 0) & (last_user(query_start) == last_user(key_start + ROWS - 1))
            key_tile = lax.dynamic_index_in_dim(key_tiles, safe_index, 0, keepdims=False)
            value_tile = lax.dynamic_index_in_dim(value_tiles, safe_index, 0, keepdims=False)
            parts = lax.cond(live, lambda: pair_task(query_tile, grad_tile, key_tile, value_tile, query_start, key_start, user_ends), lambda: zero_parts)
            query_total = query_total + parts[0].astype(jnp.float32)
            pair_acc = pair_acc.at[safe_index].add(parts[1].astype(jnp.float32))
        return (pair_acc, query_total)
    start_acc = jnp.zeros((tile_count, 2, ROWS, heads, HEAD), jnp.float32)
    pair_acc, query_totals = lax.scan(per_tile, start_acc, jnp.arange(tile_count, dtype=jnp.int32))
    query_full = query_totals.reshape(TOKENS, D).astype(jnp.bfloat16)
    pair_full = jnp.transpose(pair_acc, (1, 0, 2, 3, 4)).reshape(2, TOKENS, D).astype(jnp.bfloat16)
    d_input = jnp.dot(query_full, w_proj[0].T, preferred_element_type=jnp.float32)
    d_input = d_input + jnp.dot(pair_full[0], w_proj[1].T, preferred_element_type=jnp.float32)
    d_input = d_input + jnp.dot(pair_full[1], w_proj[2].T, preferred_element_type=jnp.float32)
    return d_input
```

```python
import functools
import math

import jax
import jax.numpy as jnp
from jax import lax
from jax.experimental import pallas as pl
from jax.experimental.pallas import tpu as pltpu
from jax.sharding import PartitionSpec as P

MAXLEN = 3072
BLOCK = 512
F32 = jnp.float32
BF16 = jnp.bfloat16
VMEM = pl.BlockSpec(memory_space=pltpu.VMEM)
SMEM = pl.BlockSpec(memory_space=pltpu.SMEM)


def shift(value, axis, by):
    count = lax.axis_size(axis)
    pairs = [(i, i + by) for i in range(count) if 0 <= i + by < count]
    return lax.ppermute(value, axis, pairs)


def swap(value, axis, bit):
    count = lax.axis_size(axis)
    return lax.ppermute(value, axis, [(i, i ^ bit) for i in range(count)])


def user_bounds(lengths_ref, position):
    def step(u, carry):
        end, first, last = carry
        end = end + lengths_ref[u]
        past = end <= position
        return (
            end,
            jnp.where(past, end, first),
            jnp.where(past, last, jnp.minimum(last, end)),
        )

    zero = jnp.int32(0)
    _, first, last = lax.fori_loop(
        0, lengths_ref.shape[0], step, (zero, zero, jnp.int32(2**30))
    )
    return first, last


def pair_limits(lengths_ref, query_start, key_start, rows):
    first, last = user_bounds(lengths_ref, query_start)
    live = first <= key_start + rows - 1
    query_rows = jnp.where(live, jnp.minimum(last - query_start, rows), 0)
    key_row = jnp.maximum(first - key_start, 0)
    return query_rows, key_row


def scores(q, g, k, v, mask=None):
    nt = (((1,), (1,)), ((), ()))
    half = lax.dot_general(k, q, nt, preferred_element_type=F32) * (0.5 * q.shape[1] ** -0.5)
    da = lax.dot_general(v, g, nt, preferred_element_type=F32)
    t = jnp.tanh(half)
    p = half * t
    a = half + p
    f = (1.0 + t) * (1.0 + (half - p)) * da
    if mask is not None:
        a = jnp.where(mask, a, 0.0)
        f = jnp.where(mask, f, 0.0)
    return a.astype(BF16), f.astype(BF16)


def add_block(qs, ks, q, g, k, v, a, f, dq_ref, dk_ref, dv_ref):
    dv_ref[ks, :] += jnp.dot(a, g, preferred_element_type=F32)
    dk_ref[ks, :] += jnp.dot(f, q, preferred_element_type=F32)
    dq_ref[qs, :] += lax.dot_general(f, k, (((0,), (0,)), ((), ())), preferred_element_type=F32)


def sweep(q_ref, g_ref, k_ref, v_ref, dq_ref, dk_ref, dv_ref, query_rows, key_row, q0=0, nq=None, k0=0, nk=None):
    width = q_ref.shape[1]
    nk = k_ref.shape[0] // BLOCK if nk is None else nk
    zero = jnp.zeros((), BF16)

    def key_block(kb, carry):
        kk = pl.multiple_of(kb * BLOCK, BLOCK)
        ks = pl.ds(kk + k0, BLOCK)
        kept_keys = lax.broadcasted_iota(jnp.int32, (BLOCK, width), 0) + kk >= key_row

        def query_block(qb, carry):
            qq = pl.multiple_of(qb * BLOCK, BLOCK)
            qs = pl.ds(qq + q0, BLOCK)
            kept = lax.broadcasted_iota(jnp.int32, (BLOCK, width), 0) + qq < query_rows
            q = jnp.where(kept, q_ref[qs, :], zero)
            g = jnp.where(kept, g_ref[qs, :], zero)
            k = jnp.where(kept_keys, k_ref[ks, :], zero)
            v = jnp.where(kept_keys, v_ref[ks, :], zero)
            a, f = scores(q, g, k, v)
            add_block(qs, ks, q, g, k, v, a, f, dq_ref, dk_ref, dv_ref)
            return carry

        return lax.fori_loop(0, (query_rows + BLOCK - 1) // BLOCK, query_block, carry)

    first = jnp.where(query_rows > 0, key_row // BLOCK, nk)
    lax.fori_loop(first, nk, key_block, 0)


def own_kernel(lengths_ref, q_ref, g_ref, k_ref, v_ref, dq_ref, dk_ref, dv_ref):
    rows = q_ref.shape[0]
    start = lax.axis_index("seq") * rows
    dq_ref[...] = jnp.zeros_like(dq_ref)
    dk_ref[...] = jnp.zeros_like(dk_ref)
    dv_ref[...] = jnp.zeros_like(dv_ref)

    def diagonal(b, carry):
        off = pl.multiple_of(b * BLOCK, BLOCK)
        rs = pl.ds(off, BLOCK)
        query = lax.broadcasted_iota(jnp.int32, (1, BLOCK), 1) + start + off

        def step(u, carry):
            end, first = carry
            end = end + lengths_ref[u]
            return end, jnp.where(end <= query, end, first)

        _, first = lax.fori_loop(
            0, lengths_ref.shape[0], step, (jnp.int32(0), jnp.zeros((1, BLOCK), jnp.int32))
        )
        key = lax.broadcasted_iota(jnp.int32, (BLOCK, BLOCK), 0) + start + off
        mask = (key <= query) & (key >= first)
        q, g, k, v = q_ref[rs, :], g_ref[rs, :], k_ref[rs, :], v_ref[rs, :]
        a, f = scores(q, g, k, v, mask)
        add_block(rs, rs, q, g, k, v, a, f, dq_ref, dk_ref, dv_ref)
        return carry

    lax.fori_loop(0, rows // BLOCK, diagonal, 0)
    for b in range(1, rows // BLOCK):
        query_rows, key_row = pair_limits(lengths_ref, start + b * BLOCK, start + (b - 1) * BLOCK, BLOCK)
        key_row = jnp.where(
            query_rows > 0, jnp.maximum(user_bounds(lengths_ref, start + b * BLOCK)[0] - start, 0), 0
        )
        sweep(
            q_ref, g_ref, k_ref, v_ref, dq_ref, dk_ref, dv_ref, query_rows, key_row,
            q0=b * BLOCK, nk=b,
        )


def far_kernel(
    lengths_ref, q_ref, g_ref, qn_ref, gn_ref, k_ref, v_ref, dq_in,
    dq_ref, dqn_ref, dkv_ref, dk_ref, dv_ref,
):
    rows, width = q_ref.shape
    me = lax.axis_index("seq")
    dq_ref[...] = dq_in[...]
    dqn_ref[...] = jnp.zeros_like(dqn_ref)
    dk_ref[...] = jnp.zeros_like(dk_ref)
    dv_ref[...] = jnp.zeros_like(dv_ref)
    key_start = (me - 2) * rows
    near = pair_limits(lengths_ref, me * rows, key_start, rows)
    sweep(q_ref, g_ref, k_ref, v_ref, dq_ref, dk_ref, dv_ref, *near)
    far = pair_limits(lengths_ref, (me + 1) * rows, key_start, rows)
    sweep(qn_ref, gn_ref, k_ref, v_ref, dqn_ref, dk_ref, dv_ref, *far)
    norm = MAXLEN**-0.5
    dkv_ref[0] = (dk_ref[...] * (0.5 * norm * width**-0.5)).astype(BF16)
    dkv_ref[1] = (dv_ref[...] * norm).astype(BF16)


def next_kernel(
    lengths_ref, qn_ref, gn_ref, k_ref, v_ref, dqn_in, dk_in, dv_in,
    dqn_out, dk_ref, dv_ref, dqn_ref,
):
    rows, width = qn_ref.shape
    me = lax.axis_index("seq")
    dqn_ref[...] = dqn_in[...]
    dk_ref[...] = dk_in[...]
    dv_ref[...] = dv_in[...]
    limits = pair_limits(lengths_ref, (me + 1) * rows, me * rows, rows)
    sweep(qn_ref, gn_ref, k_ref, v_ref, dqn_ref, dk_ref, dv_ref, *limits)
    dqn_out[...] = (dqn_ref[...] * (0.5 * MAXLEN**-0.5 * width**-0.5)).astype(BF16)


def total_kernel(dq_ref, dk_ref, dv_ref, dq_got, dkv_got, keep_ref, send_ref):
    width = dq_ref.shape[1]
    block = keep_ref.shape[0] // 2
    norm = MAXLEN**-0.5
    inner = 0.5 * norm * width**-0.5
    low = lax.axis_index("head") % 2
    for out_ref, bit in ((send_ref, 1 - low), (keep_ref, low)):
        for high in range(2):
            src = pl.ds(pl.multiple_of((2 * high + bit) * block, block), block)
            dst = pl.ds(high * block, block)
            parts = (
                dq_ref[src, :] * inner + dq_got[src, :].astype(F32),
                dk_ref[src, :] * inner + dkv_got[0, src, :].astype(F32),
                dv_ref[src, :] * norm + dkv_got[1, src, :].astype(F32),
            )
            for c, part in enumerate(parts):
                out_ref[dst, c * width : (c + 1) * width] = part.astype(BF16)


def project_kernel(keep_ref, got_ref, w_ref, wp_ref, mine_ref, send_ref):
    width = w_ref.shape[2]
    block = mine_ref.shape[0]
    high = lax.axis_index("head") // 2

    def rows_of(index):
        src = pl.ds(pl.multiple_of(index * block, block), block)
        total = None
        for grads, weights in ((keep_ref, w_ref), (got_ref, wp_ref)):
            for c in range(3):
                part = lax.dot_general(
                    grads[src, c * width : (c + 1) * width], weights[c],
                    (((1,), (1,)), ((), ())), preferred_element_type=F32,
                )
                total = part if total is None else total + part
        return total

    send_ref[...] = rows_of(1 - high).astype(BF16)
    mine_ref[...] = rows_of(high)


def call(body, name, outs, args, flops, scratch=(), lengths=True):
    specs = [SMEM if lengths and n == 0 else VMEM for n in range(len(args))]
    moved = sum(math.prod(a.shape) * a.dtype.itemsize for a in (*args, *outs))
    return pl.pallas_call(
        body,
        name=name,
        out_shape=outs,
        in_specs=specs,
        out_specs=tuple(VMEM for _ in outs),
        scratch_shapes=scratch,
        compiler_params=pltpu.CompilerParams(vmem_limit_bytes=24 * 2**20),
        cost_estimate=pl.CostEstimate(flops=flops, bytes_accessed=moved, transcendentals=0),
    )(*args)


def shards(queries, keys, values, out_grad, lengths, w_proj):
    rows, width = queries.shape
    model = w_proj.shape[1]
    heads = lax.axis_size("head")
    like = jax.ShapeDtypeStruct
    wide = like((rows, width), F32)
    pair_flops = 10 * rows * rows * width

    keys_got = shift(keys, "seq", 2)
    values_got = shift(values, "seq", 2)
    queries_got = shift(queries, "seq", -1)
    grad_got = shift(out_grad, "seq", -1)
    w_got = swap(w_proj, "head", 1)

    dq, dk, dv = call(
        own_kernel, "own", (wide, wide, wide), (lengths, queries, out_grad, keys, values), pair_flops
    )
    dq, dqn, dkv = call(
        far_kernel, "far", (wide, wide, like((2, rows, width), BF16)),
        (lengths, queries, out_grad, queries_got, grad_got, keys_got, values_got, dq),
        pair_flops,
        scratch=[pltpu.VMEM((rows, width), F32), pltpu.VMEM((rows, width), F32)],
    )
    dkv_got = shift(dkv, "seq", -2)
    dqn, dk, dv = call(
        next_kernel, "next", (like((rows, width), BF16), wide, wide),
        (lengths, queries_got, grad_got, keys, values, dqn, dk, dv),
        pair_flops,
        scratch=[pltpu.VMEM((rows, width), F32)],
    )
    dq_got = shift(dqn, "seq", 1)

    block = rows // heads
    packed = like((2 * block, 3 * width), BF16)
    keep, send = call(
        total_kernel, "total", (packed, packed), (dq, dk, dv, dq_got, dkv_got), 1000, lengths=False
    )
    got = swap(send, "head", 1)
    mine, send = call(
        project_kernel, "project", (like((block, model), F32), like((block, model), BF16)),
        (keep, got, w_proj, w_got), 12 * block * width * model, lengths=False,
    )
    return mine + swap(send, "head", 2).astype(F32)


def solution(mesh):
    return jax.shard_map(
        shards,
        mesh=mesh,
        in_specs=(
            P("seq", "head"),
            P("seq", "head"),
            P("seq", "head"),
            P("seq", "head"),
            P(),
            P(None, None, "head"),
        ),
        out_specs=P(("seq", "head"), None),
        check_vma=False,
    )
```

```python
import functools
import math

import jax
import jax.numpy as jnp
from jax import lax
from jax.experimental import pallas as pl
from jax.experimental.pallas import tpu as pltpu
from jax.sharding import PartitionSpec as P

MAXLEN = 3072
BLOCK = 512
F32 = jnp.float32
BF16 = jnp.bfloat16
VMEM = pl.BlockSpec(memory_space=pltpu.VMEM)
SMEM = pl.BlockSpec(memory_space=pltpu.SMEM)


def shift(value, by, flip=0):
    tiles, heads = lax.axis_size("seq"), lax.axis_size("head")
    pairs = [
        (t * heads + h, (t + by) * heads + (h ^ flip))
        for t in range(tiles)
        for h in range(heads)
        if 0 <= t + by < tiles
    ]
    return lax.ppermute(value, ("seq", "head"), pairs)


def user_bounds(lengths_ref, position):
    def step(u, carry):
        end, first, last = carry
        end = end + lengths_ref[u]
        past = end <= position
        return (
            end,
            jnp.where(past, end, first),
            jnp.where(past, last, jnp.minimum(last, end)),
        )

    zero = jnp.int32(0)
    _, first, last = lax.fori_loop(
        0, lengths_ref.shape[0], step, (zero, zero, jnp.int32(2**30))
    )
    return first, last


def pair_limits(lengths_ref, query_start, key_start, rows):
    first, last = user_bounds(lengths_ref, query_start)
    live = first <= key_start + rows - 1
    query_rows = jnp.where(live, jnp.minimum(last - query_start, rows), 0)
    key_row = jnp.maximum(first - key_start, 0)
    return query_rows, key_row


def scores(q, g, k, v, mask=None):
    nt = (((1,), (1,)), ((), ()))
    half = lax.dot_general(k, q, nt, preferred_element_type=F32) * (0.5 * q.shape[1] ** -0.5)
    da = lax.dot_general(v, g, nt, preferred_element_type=F32)
    t = jnp.tanh(half)
    p = half * t
    a = half + p
    f = (1.0 + t) * (1.0 + (half - p)) * da
    if mask is not None:
        a = jnp.where(mask, a, 0.0)
        f = jnp.where(mask, f, 0.0)
    return a.astype(BF16), f.astype(BF16)


def add_block(qs, ks, q, g, k, v, a, f, dq_ref, dk_ref, dv_ref):
    dv_ref[ks, :] += jnp.dot(a, g, preferred_element_type=F32)
    dk_ref[ks, :] += jnp.dot(f, q, preferred_element_type=F32)
    dq_ref[qs, :] += lax.dot_general(f, k, (((0,), (0,)), ((), ())), preferred_element_type=F32)


def sweep(q_ref, g_ref, k_ref, v_ref, dq_ref, dk_ref, dv_ref, query_rows, key_row, q0=0, nq=None, k0=0, nk=None):
    width = q_ref.shape[1]
    nk = k_ref.shape[0] // BLOCK if nk is None else nk
    zero = jnp.zeros((), BF16)

    def key_block(kb, carry):
        kk = pl.multiple_of(kb * BLOCK, BLOCK)
        ks = pl.ds(kk + k0, BLOCK)
        kept_keys = lax.broadcasted_iota(jnp.int32, (BLOCK, width), 0) + kk >= key_row

        def query_block(qb, carry):
            qq = pl.multiple_of(qb * BLOCK, BLOCK)
            qs = pl.ds(qq + q0, BLOCK)
            kept = lax.broadcasted_iota(jnp.int32, (BLOCK, width), 0) + qq < query_rows
            q = jnp.where(kept, q_ref[qs, :], zero)
            g = jnp.where(kept, g_ref[qs, :], zero)
            k = jnp.where(kept_keys, k_ref[ks, :], zero)
            v = jnp.where(kept_keys, v_ref[ks, :], zero)
            a, f = scores(q, g, k, v)
            add_block(qs, ks, q, g, k, v, a, f, dq_ref, dk_ref, dv_ref)
            return carry

        return lax.fori_loop(0, (query_rows + BLOCK - 1) // BLOCK, query_block, carry)

    first = jnp.where(query_rows > 0, key_row // BLOCK, nk)
    lax.fori_loop(first, nk, key_block, 0)


def pack_kernel(q_hbm, g_hbm, k_hbm, v_hbm, qg_ref, kv_ref, sems):
    copies = [
        pltpu.make_async_copy(q_hbm, qg_ref.at[0], sems.at[0]),
        pltpu.make_async_copy(g_hbm, qg_ref.at[1], sems.at[1]),
        pltpu.make_async_copy(k_hbm, kv_ref.at[0], sems.at[2]),
        pltpu.make_async_copy(v_hbm, kv_ref.at[1], sems.at[3]),
    ]
    for copy in copies:
        copy.start()
    for copy in copies:
        copy.wait()


def own_kernel(lengths_ref, qg_ref, kv_ref, dq_ref, dk_ref, dv_ref):
    q_ref, g_ref, k_ref, v_ref = qg_ref.at[0], qg_ref.at[1], kv_ref.at[0], kv_ref.at[1]
    rows = q_ref.shape[0]
    start = lax.axis_index("seq") * rows
    dq_ref[...] = jnp.zeros_like(dq_ref)
    dk_ref[...] = jnp.zeros_like(dk_ref)
    dv_ref[...] = jnp.zeros_like(dv_ref)

    def diagonal(b, carry):
        off = pl.multiple_of(b * BLOCK, BLOCK)
        rs = pl.ds(off, BLOCK)
        query = lax.broadcasted_iota(jnp.int32, (1, BLOCK), 1) + start + off

        def step(u, carry):
            end, first = carry
            end = end + lengths_ref[u]
            return end, jnp.where(end <= query, end, first)

        _, first = lax.fori_loop(
            0, lengths_ref.shape[0], step, (jnp.int32(0), jnp.zeros((1, BLOCK), jnp.int32))
        )
        key = lax.broadcasted_iota(jnp.int32, (BLOCK, BLOCK), 0) + start + off
        mask = (key <= query) & (key >= first)
        q, g, k, v = q_ref[rs, :], g_ref[rs, :], k_ref[rs, :], v_ref[rs, :]
        a, f = scores(q, g, k, v, mask)
        add_block(rs, rs, q, g, k, v, a, f, dq_ref, dk_ref, dv_ref)
        return carry

    lax.fori_loop(0, rows // BLOCK, diagonal, 0)
    for b in range(1, rows // BLOCK):
        query_rows, key_row = pair_limits(lengths_ref, start + b * BLOCK, start, b * BLOCK)
        query_rows = jnp.minimum(query_rows, BLOCK)
        sweep(
            q_ref, g_ref, k_ref, v_ref, dq_ref, dk_ref, dv_ref, query_rows, key_row,
            q0=b * BLOCK, nk=b,
        )


def next_kernel(lengths_ref, qgn_ref, kv_ref, dk_in, dv_in, dqn_ref, dk_ref, dv_ref):
    rows = qgn_ref.shape[1]
    me = lax.axis_index("seq")
    dqn_ref[...] = jnp.zeros_like(dqn_ref)
    dk_ref[...] = dk_in[...]
    dv_ref[...] = dv_in[...]
    limits = pair_limits(lengths_ref, (me + 1) * rows, me * rows, rows)
    sweep(
        qgn_ref.at[0], qgn_ref.at[1], kv_ref.at[0], kv_ref.at[1], dqn_ref, dk_ref, dv_ref, *limits
    )


def far_kernel(
    lengths_ref, qg_ref, qgn_ref, kv_ref, dq_in, dqn_in, dk_own, dv_own,
    keep_ref, send_ref, dq_same, dq_cross, dkv_same, dkv_cross,
    dq_ref, dqn_ref, dk_ref, dv_ref,
):
    rows, width = dq_in.shape
    me = lax.axis_index("seq")
    dq_ref[...] = dq_in[...]
    dqn_ref[...] = dqn_in[...]
    dk_ref[...] = jnp.zeros_like(dk_ref)
    dv_ref[...] = jnp.zeros_like(dv_ref)
    k_ref, v_ref = kv_ref.at[0], kv_ref.at[1]
    key_start = (me - 2) * rows
    near = pair_limits(lengths_ref, me * rows, key_start, rows)
    sweep(qg_ref.at[0], qg_ref.at[1], k_ref, v_ref, dq_ref, dk_ref, dv_ref, *near)
    far = pair_limits(lengths_ref, (me + 1) * rows, key_start, rows)
    sweep(qgn_ref.at[0], qgn_ref.at[1], k_ref, v_ref, dqn_ref, dk_ref, dv_ref, *far)

    norm = MAXLEN**-0.5
    inner = 0.5 * norm * width**-0.5
    block = dq_same.shape[0] // 2
    low = lax.axis_index("head") % 2
    for high in range(2):
        dst = pl.ds(high * block, block)
        for bit, dq_out, dkv_out, own_out in (
            (low, dq_same, dkv_same, keep_ref),
            (1 - low, dq_cross, dkv_cross, send_ref),
        ):
            src = pl.ds(pl.multiple_of((2 * high + bit) * block, block), block)
            dq_out[dst, :] = (dqn_ref[src, :] * inner).astype(BF16)
            dkv_out[0, dst, :] = (dk_ref[src, :] * inner).astype(BF16)
            dkv_out[1, dst, :] = (dv_ref[src, :] * norm).astype(BF16)
            own = (dq_ref[src, :] * inner, dk_own[src, :] * inner, dv_own[src, :] * norm)
            for c, part in enumerate(own):
                own_out[c, dst, :] = part.astype(own_out.dtype)


def project_kernel(
    keep_ref, got_ref, dq_same, dq_cross, dkv_same, dkv_cross, w_ref, wp_ref, mine_ref, send_ref
):
    block = mine_ref.shape[0]
    high = lax.axis_index("head") // 2

    def rows_of(index):
        src = pl.ds(pl.multiple_of(index * block, block), block)
        total = None
        for own, dq, dkv, weights in (
            (keep_ref, dq_same, dkv_same, w_ref),
            (got_ref, dq_cross, dkv_cross, wp_ref),
        ):
            arrived = (dq[src, :], dkv[0, src, :], dkv[1, src, :])
            for c, add in enumerate(arrived):
                grad = (own[c, src, :].astype(F32) + add.astype(F32)).astype(BF16)
                part = lax.dot_general(
                    grad, weights[c], (((1,), (1,)), ((), ())), preferred_element_type=F32
                )
                total = part if total is None else total + part
        return total

    send_ref[...] = rows_of(1 - high).astype(BF16)
    mine_ref[...] = rows_of(high)


def call(body, name, outs, args, flops, scratch=(), lengths=True, space=VMEM, limit=24):
    specs = [SMEM if lengths and n == 0 else space for n in range(len(args))]
    moved = sum(math.prod(a.shape) * a.dtype.itemsize for a in (*args, *outs))
    return pl.pallas_call(
        body,
        name=name,
        out_shape=outs,
        in_specs=specs,
        out_specs=tuple(VMEM for _ in outs),
        scratch_shapes=scratch,
        compiler_params=pltpu.CompilerParams(vmem_limit_bytes=limit * 2**20),
        cost_estimate=pl.CostEstimate(flops=flops, bytes_accessed=moved, transcendentals=0),
    )(*args)


def shards(queries, keys, values, out_grad, lengths, w_proj):
    rows, width = queries.shape
    model = w_proj.shape[1]
    heads = lax.axis_size("head")
    block = rows // heads
    like = jax.ShapeDtypeStruct
    wide = like((rows, width), F32)
    pair = like((2, rows, width), BF16)
    pair_flops = 10 * rows * rows * width

    query_grad, key_value = call(
        pack_kernel, "pack", (pair, pair), (queries, out_grad, keys, values), 1000,
        scratch=[pltpu.SemaphoreType.DMA((4,))], lengths=False,
        space=pl.BlockSpec(memory_space=pltpu.HBM), limit=60,
    )
    query_grad_got = shift(query_grad, -1)
    key_value_got = shift(key_value, 2)

    dq, dk, dv = call(
        own_kernel, "own", (wide, wide, wide), (lengths, query_grad, key_value), pair_flops
    )
    dqn, dk, dv = call(
        next_kernel, "next", (wide, wide, wide),
        (lengths, query_grad_got, key_value, dk, dv), pair_flops,
    )
    keep, send, dq_same, dq_cross, dkv_same, dkv_cross = call(
        far_kernel, "far",
        (
            like((3, 2 * block, width), F32), like((3, 2 * block, width), BF16),
            like((2 * block, width), BF16), like((2 * block, width), BF16),
            like((2, 2 * block, width), BF16), like((2, 2 * block, width), BF16),
        ),
        (lengths, query_grad, query_grad_got, key_value_got, dq, dqn, dk, dv),
        pair_flops,
        scratch=[pltpu.VMEM((rows, width), F32)] * 4,
    )
    dkv_same = shift(dkv_same, -2)
    dkv_cross = shift(dkv_cross, -2, 1)
    dq_same = shift(dq_same, 1)
    dq_cross = shift(dq_cross, 1, 1)
    got = shift(send, 0, 1)
    w_got = shift(w_proj, 0, 1)

    mine, send = call(
        project_kernel, "project", (like((block, model), F32), like((block, model), BF16)),
        (keep, got, dq_same, dq_cross, dkv_same, dkv_cross, w_proj, w_got),
        12 * block * width * model, lengths=False,
    )
    return mine + shift(send, 0, 2).astype(F32)


def solution(mesh):
    return jax.shard_map(
        shards,
        mesh=mesh,
        in_specs=(
            P("seq", "head"),
            P("seq", "head"),
            P("seq", "head"),
            P("seq", "head"),
            P(),
            P(None, None, "head"),
        ),
        out_specs=P(("seq", "head"), None),
        check_vma=False,
    )
```

```python
import functools
import math

import jax
import jax.numpy as jnp
from jax import lax
from jax.experimental import pallas as pl
from jax.experimental.pallas import tpu as pltpu
from jax.sharding import PartitionSpec as P

MAXLEN = 3072
BLOCK = 512
F32 = jnp.float32
BF16 = jnp.bfloat16
VMEM = pl.BlockSpec(memory_space=pltpu.VMEM)
SMEM = pl.BlockSpec(memory_space=pltpu.SMEM)


def shift(value, by, flip=0):
    tiles, heads = lax.axis_size("seq"), lax.axis_size("head")
    pairs = [
        (t * heads + h, (t + by) * heads + (h ^ flip))
        for t in range(tiles)
        for h in range(heads)
        if 0 <= t + by < tiles
    ]
    return lax.ppermute(value, ("seq", "head"), pairs)


def user_bounds(lengths_ref, position):
    def step(u, carry):
        end, first, last = carry
        end = end + lengths_ref[u]
        past = end <= position
        return (
            end,
            jnp.where(past, end, first),
            jnp.where(past, last, jnp.minimum(last, end)),
        )

    zero = jnp.int32(0)
    _, first, last = lax.fori_loop(
        0, lengths_ref.shape[0], step, (zero, zero, jnp.int32(2**30))
    )
    return first, last


def pair_limits(lengths_ref, query_start, key_start, rows):
    first, last = user_bounds(lengths_ref, query_start)
    live = first <= key_start + rows - 1
    query_rows = jnp.where(live, jnp.minimum(last - query_start, rows), 0)
    key_row = jnp.maximum(first - key_start, 0)
    return query_rows, key_row


def scores(q, g, k, v, mask=None):
    nt = (((1,), (1,)), ((), ()))
    half = lax.dot_general(k, q, nt, preferred_element_type=F32) * (0.5 * q.shape[1] ** -0.5)
    da = lax.dot_general(v, g, nt, preferred_element_type=F32)
    t = jnp.tanh(half)
    p = half * t
    a = half + p
    f = (1.0 + t) * (1.0 + (half - p)) * da
    if mask is not None:
        a = jnp.where(mask, a, 0.0)
        f = jnp.where(mask, f, 0.0)
    return a.astype(BF16), f.astype(BF16)


def add_block(qs, ks, q, g, k, v, a, f, dq_ref, dk_ref, dv_ref):
    dv_ref[ks, :] += jnp.dot(a, g, preferred_element_type=F32)
    dk_ref[ks, :] += jnp.dot(f, q, preferred_element_type=F32)
    dq_ref[qs, :] += lax.dot_general(f, k, (((0,), (0,)), ((), ())), preferred_element_type=F32)


def sweep(q_ref, g_ref, k_ref, v_ref, dq_ref, dk_ref, dv_ref, query_rows, key_row, q0=0, nq=None, k0=0, nk=None):
    width = q_ref.shape[1]
    nk = k_ref.shape[0] // BLOCK if nk is None else nk
    zero = jnp.zeros((), BF16)

    def key_block(kb, carry):
        kk = pl.multiple_of(kb * BLOCK, BLOCK)
        ks = pl.ds(kk + k0, BLOCK)
        kept_keys = lax.broadcasted_iota(jnp.int32, (BLOCK, width), 0) + kk >= key_row

        def query_block(qb, carry):
            qq = pl.multiple_of(qb * BLOCK, BLOCK)
            qs = pl.ds(qq + q0, BLOCK)
            kept = lax.broadcasted_iota(jnp.int32, (BLOCK, width), 0) + qq < query_rows
            q = jnp.where(kept, q_ref[qs, :], zero)
            g = jnp.where(kept, g_ref[qs, :], zero)
            k = jnp.where(kept_keys, k_ref[ks, :], zero)
            v = jnp.where(kept_keys, v_ref[ks, :], zero)
            a, f = scores(q, g, k, v)
            add_block(qs, ks, q, g, k, v, a, f, dq_ref, dk_ref, dv_ref)
            return carry

        return lax.fori_loop(0, (query_rows + BLOCK - 1) // BLOCK, query_block, carry)

    first = jnp.where(query_rows > 0, key_row // BLOCK, nk)
    lax.fori_loop(first, nk, key_block, 0)


def pack_kernel(q_hbm, g_hbm, k_hbm, v_hbm, qg_ref, kv_ref, sems):
    copies = [
        pltpu.make_async_copy(q_hbm, qg_ref.at[0], sems.at[0]),
        pltpu.make_async_copy(g_hbm, qg_ref.at[1], sems.at[1]),
        pltpu.make_async_copy(k_hbm, kv_ref.at[0], sems.at[2]),
        pltpu.make_async_copy(v_hbm, kv_ref.at[1], sems.at[3]),
    ]
    for copy in copies:
        copy.start()
    for copy in copies:
        copy.wait()


def own_kernel(lengths_ref, qg_ref, kv_ref, dq_ref, dk_ref, dv_ref):
    q_ref, g_ref, k_ref, v_ref = qg_ref.at[0], qg_ref.at[1], kv_ref.at[0], kv_ref.at[1]
    rows = q_ref.shape[0]
    start = lax.axis_index("seq") * rows
    dq_ref[...] = jnp.zeros_like(dq_ref)
    dk_ref[...] = jnp.zeros_like(dk_ref)
    dv_ref[...] = jnp.zeros_like(dv_ref)

    def diagonal(b, carry):
        off = pl.multiple_of(b * BLOCK, BLOCK)
        rs = pl.ds(off, BLOCK)
        query = lax.broadcasted_iota(jnp.int32, (1, BLOCK), 1) + start + off

        def step(u, carry):
            end, first = carry
            end = end + lengths_ref[u]
            return end, jnp.where(end <= query, end, first)

        _, first = lax.fori_loop(
            0, lengths_ref.shape[0], step, (jnp.int32(0), jnp.zeros((1, BLOCK), jnp.int32))
        )
        key = lax.broadcasted_iota(jnp.int32, (BLOCK, BLOCK), 0) + start + off
        mask = (key <= query) & (key >= first)
        q, g, k, v = q_ref[rs, :], g_ref[rs, :], k_ref[rs, :], v_ref[rs, :]
        a, f = scores(q, g, k, v, mask)
        add_block(rs, rs, q, g, k, v, a, f, dq_ref, dk_ref, dv_ref)
        return carry

    lax.fori_loop(0, rows // BLOCK, diagonal, 0)
    for b in range(1, rows // BLOCK):
        query_rows, key_row = pair_limits(lengths_ref, start + b * BLOCK, start, b * BLOCK)
        query_rows = jnp.minimum(query_rows, BLOCK)
        sweep(
            q_ref, g_ref, k_ref, v_ref, dq_ref, dk_ref, dv_ref, query_rows, key_row,
            q0=b * BLOCK, nk=b,
        )


def next_kernel(lengths_ref, qgn_ref, kv_ref, dk_in, dv_in, dqn_ref, dk_ref, dv_ref):
    rows = qgn_ref.shape[1]
    me = lax.axis_index("seq")
    dqn_ref[...] = jnp.zeros_like(dqn_ref)
    dk_ref[...] = dk_in[...]
    dv_ref[...] = dv_in[...]
    limits = pair_limits(lengths_ref, (me + 1) * rows, me * rows, rows)
    sweep(
        qgn_ref.at[0], qgn_ref.at[1], kv_ref.at[0], kv_ref.at[1], dqn_ref, dk_ref, dv_ref, *limits
    )


def far_kernel(
    lengths_ref, qg_ref, qgn_ref, kv_ref, dq_in, dqn_in, dk_own, dv_own,
    keep_ref, send_ref, dq_same, dq_cross, dkv_same, dkv_cross,
    dq_ref, dqn_ref, dk_ref, dv_ref,
):
    rows, width = dq_in.shape
    me = lax.axis_index("seq")
    dq_ref[...] = dq_in[...]
    dqn_ref[...] = dqn_in[...]
    dk_ref[...] = jnp.zeros_like(dk_ref)
    dv_ref[...] = jnp.zeros_like(dv_ref)
    k_ref, v_ref = kv_ref.at[0], kv_ref.at[1]
    key_start = (me - 2) * rows
    near = pair_limits(lengths_ref, me * rows, key_start, rows)
    sweep(qg_ref.at[0], qg_ref.at[1], k_ref, v_ref, dq_ref, dk_ref, dv_ref, *near)
    far = pair_limits(lengths_ref, (me + 1) * rows, key_start, rows)
    sweep(qgn_ref.at[0], qgn_ref.at[1], k_ref, v_ref, dqn_ref, dk_ref, dv_ref, *far)

    norm = MAXLEN**-0.5
    inner = 0.5 * norm * width**-0.5
    block = dq_same.shape[0] // 2
    low = lax.axis_index("head") % 2
    for high in range(2):
        dst = pl.ds(high * block, block)
        for bit, dq_out, dkv_out, own_out in (
            (low, dq_same, dkv_same, keep_ref),
            (1 - low, dq_cross, dkv_cross, send_ref),
        ):
            src = pl.ds(pl.multiple_of((2 * high + bit) * block, block), block)
            dq_out[dst, :] = (dqn_ref[src, :] * inner).astype(BF16)
            dkv_out[0, dst, :] = (dk_ref[src, :] * inner).astype(BF16)
            dkv_out[1, dst, :] = (dv_ref[src, :] * norm).astype(BF16)
            own = (dq_ref[src, :] * inner, dk_own[src, :] * inner, dv_own[src, :] * norm)
            for c, part in enumerate(own):
                own_out[c, dst, :] = part.astype(own_out.dtype)


def project_kernel(
    keep_ref, got_ref, dq_same, dq_cross, dkv_same, dkv_cross, w_ref, wp_ref, mine_ref, send_ref
):
    block = mine_ref.shape[0]
    high = lax.axis_index("head") // 2

    def rows_of(index):
        src = pl.ds(pl.multiple_of(index * block, block), block)
        total = None
        for own, dq, dkv, weights in (
            (keep_ref, dq_same, dkv_same, w_ref),
            (got_ref, dq_cross, dkv_cross, wp_ref),
        ):
            arrived = (dq[src, :], dkv[0, src, :], dkv[1, src, :])
            for c, add in enumerate(arrived):
                grad = (own[c, src, :].astype(F32) + add.astype(F32)).astype(BF16)
                part = lax.dot_general(
                    grad, weights[c], (((1,), (1,)), ((), ())), preferred_element_type=F32
                )
                total = part if total is None else total + part
        return total

    send_ref[...] = rows_of(1 - high).astype(BF16)
    mine_ref[...] = rows_of(high)


def call(body, name, outs, args, flops, scratch=(), lengths=True, space=VMEM, limit=24):
    specs = [SMEM if lengths and n == 0 else space for n in range(len(args))]
    moved = sum(math.prod(a.shape) * a.dtype.itemsize for a in (*args, *outs))
    return pl.pallas_call(
        body,
        name=name,
        out_shape=outs,
        in_specs=specs,
        out_specs=tuple(VMEM for _ in outs),
        scratch_shapes=scratch,
        compiler_params=pltpu.CompilerParams(vmem_limit_bytes=limit * 2**20),
        cost_estimate=pl.CostEstimate(flops=flops, bytes_accessed=moved, transcendentals=0),
    )(*args)


def shards(queries, keys, values, out_grad, lengths, w_proj):
    rows, width = queries.shape
    model = w_proj.shape[1]
    heads = lax.axis_size("head")
    block = rows // heads
    like = jax.ShapeDtypeStruct
    wide = like((rows, width), F32)
    pair = like((2, rows, width), BF16)
    pair_flops = 10 * rows * rows * width

    query_grad, key_value = call(
        pack_kernel, "pack", (pair, pair), tuple(pltpu.with_memory_space_constraint(x, pltpu.HBM) for x in (queries, out_grad, keys, values)), 1000,
        scratch=[pltpu.SemaphoreType.DMA((4,))], lengths=False,
        space=pl.BlockSpec(memory_space=pltpu.HBM),
    )
    query_grad_got = shift(query_grad, -1)
    key_value_got = shift(key_value, 2)

    dq, dk, dv = call(
        own_kernel, "own", (wide, wide, wide), (lengths, query_grad, key_value), pair_flops
    )
    dqn, dk, dv = call(
        next_kernel, "next", (wide, wide, wide),
        (lengths, query_grad_got, key_value, dk, dv), pair_flops,
    )
    keep, send, dq_same, dq_cross, dkv_same, dkv_cross = call(
        far_kernel, "far",
        (
            like((3, 2 * block, width), F32), like((3, 2 * block, width), BF16),
            like((2 * block, width), BF16), like((2 * block, width), BF16),
            like((2, 2 * block, width), BF16), like((2, 2 * block, width), BF16),
        ),
        (lengths, query_grad, query_grad_got, key_value_got, dq, dqn, dk, dv),
        pair_flops,
        scratch=[pltpu.VMEM((rows, width), F32)] * 4,
    )
    dkv_same = shift(dkv_same, -2)
    dkv_cross = shift(dkv_cross, -2, 1)
    dq_same = shift(dq_same, 1)
    dq_cross = shift(dq_cross, 1, 1)
    got = shift(send, 0, 1)
    w_got = shift(w_proj, 0, 1)

    mine, send = call(
        project_kernel, "project", (like((block, model), F32), like((block, model), BF16)),
        (keep, got, dq_same, dq_cross, dkv_same, dkv_cross, w_proj, w_got),
        12 * block * width * model, lengths=False,
    )
    return mine + shift(send, 0, 2).astype(F32)


def solution(mesh):
    return jax.shard_map(
        shards,
        mesh=mesh,
        in_specs=(
            P("seq", "head"),
            P("seq", "head"),
            P("seq", "head"),
            P("seq", "head"),
            P(),
            P(None, None, "head"),
        ),
        out_specs=P(("seq", "head"), None),
        check_vma=False,
    )
```

```python
import math

import jax
import jax.numpy as jnp
from jax import lax
from jax.experimental import pallas as pl
from jax.experimental.pallas import tpu as pltpu
from jax.sharding import PartitionSpec as P


MAXLEN = 3072
BLOCK = 512
F32 = jnp.float32
BF16 = jnp.bfloat16
VMEM = pl.BlockSpec(memory_space=pltpu.VMEM)
SMEM = pl.BlockSpec(memory_space=pltpu.SMEM)


def shift(value, by, flip=0):
    tiles, heads = lax.axis_size("seq"), lax.axis_size("head")
    pairs = [
        (t * heads + h, (t + by) * heads + (h ^ flip))
        for t in range(tiles)
        for h in range(heads)
        if 0 <= t + by < tiles
    ]
    return lax.ppermute(value, ("seq", "head"), pairs)


def user_bounds(lengths_ref, position):
    def step(u, carry):
        end, first, last = carry
        end = end + lengths_ref[u]
        past = end <= position
        return (
            end,
            jnp.where(past, end, first),
            jnp.where(past, last, jnp.minimum(last, end)),
        )

    zero = jnp.int32(0)
    _, first, last = lax.fori_loop(
        0, lengths_ref.shape[0], step, (zero, zero, jnp.int32(2**30))
    )
    return first, last


def pair_limits(lengths_ref, query_start, key_start, rows):
    first, last = user_bounds(lengths_ref, query_start)
    live = first <= key_start + rows - 1
    query_rows = jnp.where(live, jnp.minimum(last - query_start, rows), 0)
    key_row = jnp.maximum(first - key_start, 0)
    return query_rows, key_row


def scores(q, g, k, v, mask=None):
    nt = (((1,), (1,)), ((), ()))
    half = lax.dot_general(k, q, nt, preferred_element_type=F32) * (0.5 * q.shape[1] ** -0.5)
    da = lax.dot_general(v, g, nt, preferred_element_type=F32)
    t = jnp.tanh(half)
    p = half * t
    a = half + p
    f = (1.0 + t) * (1.0 + (half - p)) * da
    if mask is not None:
        a = jnp.where(mask, a, 0.0)
        f = jnp.where(mask, f, 0.0)
    return a.astype(BF16), f.astype(BF16)


def add_block(qs, ks, q, g, k, a, f, dq_ref, dk_ref, dv_ref):
    dv_ref[ks, :] += jnp.dot(a, g, preferred_element_type=F32)
    dk_ref[ks, :] += jnp.dot(f, q, preferred_element_type=F32)
    dq_ref[qs, :] += lax.dot_general(f, k, (((0,), (0,)), ((), ())), preferred_element_type=F32)


def sweep(q_ref, g_ref, k_ref, v_ref, dq_ref, dk_ref, dv_ref, query_rows, key_row, q0=0, nq=None, k0=0, nk=None):
    width = q_ref.shape[1]
    nk = k_ref.shape[0] // BLOCK if nk is None else nk
    zero = jnp.zeros((), BF16)

    def key_block(kb, carry):
        kk = pl.multiple_of(kb * BLOCK, BLOCK)
        ks = pl.ds(kk + k0, BLOCK)
        kept_keys = lax.broadcasted_iota(jnp.int32, (BLOCK, width), 0) + kk >= key_row

        def query_block(qb, carry):
            qq = pl.multiple_of(qb * BLOCK, BLOCK)
            qs = pl.ds(qq + q0, BLOCK)
            kept = lax.broadcasted_iota(jnp.int32, (BLOCK, width), 0) + qq < query_rows
            q = jnp.where(kept, q_ref[qs, :], zero)
            g = jnp.where(kept, g_ref[qs, :], zero)
            k = jnp.where(kept_keys, k_ref[ks, :], zero)
            v = jnp.where(kept_keys, v_ref[ks, :], zero)
            a, f = scores(q, g, k, v)
            add_block(qs, ks, q, g, k, a, f, dq_ref, dk_ref, dv_ref)
            return carry

        return lax.fori_loop(0, (query_rows + BLOCK - 1) // BLOCK, query_block, carry)

    first = jnp.where(query_rows > 0, key_row // BLOCK, nk)
    lax.fori_loop(first, nk, key_block, 0)


def pack_kernel(q_hbm, g_hbm, k_hbm, v_hbm, qg_ref, kv_ref, sems):
    copies = [
        pltpu.make_async_copy(q_hbm, qg_ref.at[0], sems.at[0]),
        pltpu.make_async_copy(g_hbm, qg_ref.at[1], sems.at[1]),
        pltpu.make_async_copy(k_hbm, kv_ref.at[0], sems.at[2]),
        pltpu.make_async_copy(v_hbm, kv_ref.at[1], sems.at[3]),
    ]
    for copy in copies:
        copy.start()
    for copy in copies:
        copy.wait()


def own_kernel(lengths_ref, qg_ref, kv_ref, dq_ref, dk_ref, dv_ref):
    q_ref, g_ref, k_ref, v_ref = qg_ref.at[0], qg_ref.at[1], kv_ref.at[0], kv_ref.at[1]
    rows = q_ref.shape[0]
    start = lax.axis_index("seq") * rows
    dq_ref[...] = jnp.zeros_like(dq_ref)
    dk_ref[...] = jnp.zeros_like(dk_ref)
    dv_ref[...] = jnp.zeros_like(dv_ref)

    def diagonal(b, carry):
        off = pl.multiple_of(b * BLOCK, BLOCK)
        rs = pl.ds(off, BLOCK)
        query = lax.broadcasted_iota(jnp.int32, (1, BLOCK), 1) + start + off

        def step(u, carry):
            end, first = carry
            end = end + lengths_ref[u]
            return end, jnp.where(end <= query, end, first)

        _, first = lax.fori_loop(
            0, lengths_ref.shape[0], step, (jnp.int32(0), jnp.zeros((1, BLOCK), jnp.int32))
        )
        key = lax.broadcasted_iota(jnp.int32, (BLOCK, BLOCK), 0) + start + off
        mask = (key <= query) & (key >= first)
        q, g, k, v = q_ref[rs, :], g_ref[rs, :], k_ref[rs, :], v_ref[rs, :]
        a, f = scores(q, g, k, v, mask)
        add_block(rs, rs, q, g, k, a, f, dq_ref, dk_ref, dv_ref)
        return carry

    lax.fori_loop(0, rows // BLOCK, diagonal, 0)
    for b in range(1, rows // BLOCK):
        query_rows, key_row = pair_limits(lengths_ref, start + b * BLOCK, start, b * BLOCK)
        query_rows = jnp.minimum(query_rows, BLOCK)
        sweep(
            q_ref, g_ref, k_ref, v_ref, dq_ref, dk_ref, dv_ref, query_rows, key_row,
            q0=b * BLOCK, nk=b,
        )


def next_kernel(lengths_ref, qgn_ref, kv_ref, dk_in, dv_in, dqn_ref, dk_ref, dv_ref):
    rows = qgn_ref.shape[1]
    me = lax.axis_index("seq")
    dqn_ref[...] = jnp.zeros_like(dqn_ref)
    dk_ref[...] = dk_in[...]
    dv_ref[...] = dv_in[...]
    limits = pair_limits(lengths_ref, (me + 1) * rows, me * rows, rows)
    sweep(
        qgn_ref.at[0], qgn_ref.at[1], kv_ref.at[0], kv_ref.at[1], dqn_ref, dk_ref, dv_ref, *limits
    )


def far_kernel(
    lengths_ref, qg_ref, qgn_ref, kv_ref, dq_in, dqn_in, dk_own, dv_own,
    keep_ref, send_ref, dq_same, dq_cross, dkv_same, dkv_cross,
    dq_ref, dqn_ref, dk_ref, dv_ref,
):
    rows, width = dq_in.shape
    me = lax.axis_index("seq")
    dq_ref[...] = dq_in[...]
    dqn_ref[...] = dqn_in[...]
    dk_ref[...] = jnp.zeros_like(dk_ref)
    dv_ref[...] = jnp.zeros_like(dv_ref)
    k_ref, v_ref = kv_ref.at[0], kv_ref.at[1]
    key_start = (me - 2) * rows
    near = pair_limits(lengths_ref, me * rows, key_start, rows)
    sweep(qg_ref.at[0], qg_ref.at[1], k_ref, v_ref, dq_ref, dk_ref, dv_ref, *near)
    far = pair_limits(lengths_ref, (me + 1) * rows, key_start, rows)
    sweep(qgn_ref.at[0], qgn_ref.at[1], k_ref, v_ref, dqn_ref, dk_ref, dv_ref, *far)

    norm = MAXLEN**-0.5
    inner = 0.5 * norm * width**-0.5
    half = dq_same.shape[0]
    block = half // 2
    head = lax.axis_index("head")
    high, low = head // 2, head % 2
    for bit, dq_out, dkv_out in ((high, dq_same, dkv_same), (1 - high, dq_cross, dkv_cross)):
        src = pl.ds(pl.multiple_of(bit * half, half), half)
        dq_out[...] = (dqn_ref[src, :] * inner).astype(BF16)
        dkv_out[0] = (dk_ref[src, :] * inner).astype(BF16)
        dkv_out[1] = (dv_ref[src, :] * norm).astype(BF16)
    for bit, out_ref in ((low, keep_ref), (1 - low, send_ref)):
        for top in range(2):
            src = pl.ds(pl.multiple_of((2 * top + bit) * block, block), block)
            dst = pl.ds(top * block, block)
            own = (dq_ref[src, :] * inner, dk_own[src, :] * inner, dv_own[src, :] * norm)
            for c, part in enumerate(own):
                out_ref[c, dst, :] = part.astype(BF16)


def project(grads, weights, total=None):
    for grad, weight in zip(grads, weights):
        part = lax.dot_general(
            grad, weight, (((1,), (1,)), ((), ())), preferred_element_type=F32
        )
        total = part if total is None else total + part
    return total


def local_kernel(keep_ref, got_ref, w_ref, w1_ref, mine_ref, send_ref):
    block = mine_ref.shape[0]
    high = lax.axis_index("head") // 2
    weights = [ref[c] for ref in (w_ref, w1_ref) for c in range(3)]
    for bit, out_ref in ((1 - high, send_ref), (high, mine_ref)):
        src = pl.ds(pl.multiple_of(bit * block, block), block)
        grads = [ref[c, src, :] for ref in (keep_ref, got_ref) for c in range(3)]
        out_ref[...] = project(grads, weights).astype(out_ref.dtype)


def split_kernel(dq_same, dkv_same, dq_cross, dkv_cross, keep_ref, send_ref):
    block = keep_ref.shape[2]
    low = lax.axis_index("head") % 2
    for bit, out_ref in ((1 - low, send_ref), (low, keep_ref)):
        src = pl.ds(pl.multiple_of(bit * block, block), block)
        for n, (dq, dkv) in enumerate(((dq_same, dkv_same), (dq_cross, dkv_cross))):
            out_ref[n, 0] = dq[src, :]
            out_ref[n, 1] = dkv[0, src, :]
            out_ref[n, 2] = dkv[1, src, :]


def final_kernel(keep_ref, got_ref, mine_ref, arrived_ref, w_ref, w1_ref, w2_ref, w3_ref, out_ref):
    grads, weights = [], []
    for half_ref, pair in ((keep_ref, (w_ref, w2_ref)), (got_ref, (w1_ref, w3_ref))):
        for n, weight in enumerate(pair):
            grads += [half_ref[n, c] for c in range(3)]
            weights += [weight[c] for c in range(3)]
    out_ref[...] = project(grads, weights, mine_ref[...] + arrived_ref[...].astype(F32))


def call(body, outs, args, flops, scratch=(), lengths=True, space=VMEM, limit=24):
    specs = [SMEM if lengths and n == 0 else space for n in range(len(args))]
    moved = sum(math.prod(a.shape) * a.dtype.itemsize for a in (*args, *outs))
    return pl.pallas_call(
        body,
        out_shape=outs,
        in_specs=specs,
        out_specs=tuple(VMEM for _ in outs),
        scratch_shapes=scratch,
        compiler_params=pltpu.CompilerParams(vmem_limit_bytes=limit * 2**20),
        cost_estimate=pl.CostEstimate(flops=flops, bytes_accessed=moved, transcendentals=0),
    )(*args)


def shards(queries, keys, values, out_grad, lengths, w_proj):
    rows, width = queries.shape
    model = w_proj.shape[1]
    heads = lax.axis_size("head")
    block = rows // heads
    like = jax.ShapeDtypeStruct
    wide = like((rows, width), F32)
    pair = like((2, rows, width), BF16)
    pair_flops = 10 * rows * rows * width

    query_grad, key_value = call(
        pack_kernel, (pair, pair), tuple(pltpu.with_memory_space_constraint(x, pltpu.HBM) for x in (queries, out_grad, keys, values)), 1000,
        scratch=[pltpu.SemaphoreType.DMA((4,))], lengths=False,
        space=pl.BlockSpec(memory_space=pltpu.HBM),
    )
    query_grad_got = shift(query_grad, -1)
    key_value_got = shift(key_value, 2)
    w1, w2, w3 = (shift(w_proj, 0, flip) for flip in (1, 2, 3))

    dq, dk, dv = call(own_kernel, (wide, wide, wide), (lengths, query_grad, key_value), pair_flops)
    dqn, dk, dv = call(
        next_kernel, (wide, wide, wide),
        (lengths, query_grad_got, key_value, dk, dv), pair_flops,
    )
    keep, send, dq_same, dq_cross, dkv_same, dkv_cross = call(
        far_kernel,
        (
            like((3, 2 * block, width), BF16), like((3, 2 * block, width), BF16),
            like((2 * block, width), BF16), like((2 * block, width), BF16),
            like((2, 2 * block, width), BF16), like((2, 2 * block, width), BF16),
        ),
        (lengths, query_grad, query_grad_got, key_value_got, dq, dqn, dk, dv),
        pair_flops,
        scratch=[pltpu.VMEM((rows, width), F32)] * 4,
    )
    dkv_cross = shift(dkv_cross, -2, 2)
    dkv_same = shift(dkv_same, -2)
    dq_cross = shift(dq_cross, 1, 2)
    dq_same = shift(dq_same, 1)
    got = shift(send, 0, 1)
    mine, send = call(
        local_kernel, (like((block, model), F32), like((block, model), BF16)),
        (keep, got, w_proj, w1), 12 * block * width * model, lengths=False,
    )
    arrived = shift(send, 0, 2)

    quarter = like((2, 3, block, width), BF16)
    keep, send = call(
        split_kernel, (quarter, quarter), (dq_same, dkv_same, dq_cross, dkv_cross), 1000,
        lengths=False,
    )
    got = shift(send, 0, 1)
    (out,) = call(
        final_kernel, (like((block, model), F32),),
        (keep, got, mine, arrived, w_proj, w1, w2, w3), 24 * block * width * model, lengths=False,
    )
    return out


def solution(mesh):
    return jax.shard_map(
        shards,
        mesh=mesh,
        in_specs=(
            P("seq", "head"),
            P("seq", "head"),
            P("seq", "head"),
            P("seq", "head"),
            P(),
            P(None, None, "head"),
        ),
        out_specs=P(("seq", "head"), None),
        check_vma=False,
    )
```

```python
import math

import jax
import jax.numpy as jnp
from jax import lax
from jax.experimental import pallas as pl
from jax.experimental.pallas import tpu as pltpu
from jax.sharding import PartitionSpec as P


MAXLEN = 3072
BLOCK = 512
F32 = jnp.float32
BF16 = jnp.bfloat16
VMEM = pl.BlockSpec(memory_space=pltpu.VMEM)
SMEM = pl.BlockSpec(memory_space=pltpu.SMEM)


def shift(value, by, flip=0):
    tiles, heads = lax.axis_size("seq"), lax.axis_size("head")
    pairs = [
        (t * heads + h, (t + by) * heads + (h ^ flip))
        for t in range(tiles)
        for h in range(heads)
        if 0 <= t + by < tiles
    ]
    return lax.ppermute(value, ("seq", "head"), pairs)


def user_bounds(lengths_ref, position):
    def step(u, carry):
        end, first, last = carry
        end = end + lengths_ref[u]
        past = end <= position
        return (
            end,
            jnp.where(past, end, first),
            jnp.where(past, last, jnp.minimum(last, end)),
        )

    zero = jnp.int32(0)
    _, first, last = lax.fori_loop(
        0, lengths_ref.shape[0], step, (zero, zero, jnp.int32(2**30))
    )
    return first, last


def pair_limits(lengths_ref, query_start, key_start, rows):
    first, last = user_bounds(lengths_ref, query_start)
    live = first <= key_start + rows - 1
    query_rows = jnp.where(live, jnp.minimum(last - query_start, rows), 0)
    key_row = jnp.maximum(first - key_start, 0)
    return query_rows, key_row


def scores(q, g, k, v, mask=None):
    nt = (((1,), (1,)), ((), ()))
    half = lax.dot_general(k, q, nt, preferred_element_type=F32) * (0.5 * q.shape[1] ** -0.5)
    da = lax.dot_general(v, g, nt, preferred_element_type=F32)
    t = jnp.tanh(half)
    p = half * t
    a = half + p
    f = (1.0 + t) * (1.0 + (half - p)) * da
    if mask is not None:
        a = jnp.where(mask, a, 0.0)
        f = jnp.where(mask, f, 0.0)
    return a.astype(BF16), f.astype(BF16)


def add_block(qs, ks, q, g, k, a, f, dq_ref, dk_ref, dv_ref):
    dv_ref[ks, :] += jnp.dot(a, g, preferred_element_type=F32)
    dk_ref[ks, :] += jnp.dot(f, q, preferred_element_type=F32)
    dq_ref[qs, :] += lax.dot_general(f, k, (((0,), (0,)), ((), ())), preferred_element_type=F32)


def sweep(q_ref, g_ref, k_ref, v_ref, dq_ref, dk_ref, dv_ref, query_rows, key_row, q0=0, nq=None, k0=0, nk=None):
    width = q_ref.shape[1]
    nk = k_ref.shape[0] // BLOCK if nk is None else nk
    zero = jnp.zeros((), BF16)

    def key_block(kb, carry):
        kk = pl.multiple_of(kb * BLOCK, BLOCK)
        ks = pl.ds(kk + k0, BLOCK)
        kept_keys = lax.broadcasted_iota(jnp.int32, (BLOCK, width), 0) + kk >= key_row

        def query_block(qb, carry):
            qq = pl.multiple_of(qb * BLOCK, BLOCK)
            qs = pl.ds(qq + q0, BLOCK)
            kept = lax.broadcasted_iota(jnp.int32, (BLOCK, width), 0) + qq < query_rows
            q = jnp.where(kept, q_ref[qs, :], zero)
            g = jnp.where(kept, g_ref[qs, :], zero)
            k = jnp.where(kept_keys, k_ref[ks, :], zero)
            v = jnp.where(kept_keys, v_ref[ks, :], zero)
            a, f = scores(q, g, k, v)
            add_block(qs, ks, q, g, k, a, f, dq_ref, dk_ref, dv_ref)
            return carry

        return lax.fori_loop(0, (query_rows + BLOCK - 1) // BLOCK, query_block, carry)

    first = jnp.where(query_rows > 0, key_row // BLOCK, nk)
    lax.fori_loop(first, nk, key_block, 0)


def pack_kernel(q_hbm, g_hbm, k_hbm, v_hbm, qg_ref, kv_ref, sems):
    copies = [
        pltpu.make_async_copy(q_hbm, qg_ref.at[0], sems.at[0]),
        pltpu.make_async_copy(g_hbm, qg_ref.at[1], sems.at[1]),
        pltpu.make_async_copy(k_hbm, kv_ref.at[0], sems.at[2]),
        pltpu.make_async_copy(v_hbm, kv_ref.at[1], sems.at[3]),
    ]
    for copy in copies:
        copy.start()
    for copy in copies:
        copy.wait()


def own_kernel(lengths_ref, qg_ref, kv_ref, dq_ref, dk_ref, dv_ref):
    q_ref, g_ref, k_ref, v_ref = qg_ref.at[0], qg_ref.at[1], kv_ref.at[0], kv_ref.at[1]
    rows = q_ref.shape[0]
    start = lax.axis_index("seq") * rows
    dq_ref[...] = jnp.zeros_like(dq_ref)
    dk_ref[...] = jnp.zeros_like(dk_ref)
    dv_ref[...] = jnp.zeros_like(dv_ref)

    def diagonal(b, carry):
        off = pl.multiple_of(b * BLOCK, BLOCK)
        rs = pl.ds(off, BLOCK)
        query = lax.broadcasted_iota(jnp.int32, (1, BLOCK), 1) + start + off

        def step(u, carry):
            end, first = carry
            end = end + lengths_ref[u]
            return end, jnp.where(end <= query, end, first)

        _, first = lax.fori_loop(
            0, lengths_ref.shape[0], step, (jnp.int32(0), jnp.zeros((1, BLOCK), jnp.int32))
        )
        key = lax.broadcasted_iota(jnp.int32, (BLOCK, BLOCK), 0) + start + off
        mask = (key <= query) & (key >= first)
        q, g, k, v = q_ref[rs, :], g_ref[rs, :], k_ref[rs, :], v_ref[rs, :]
        a, f = scores(q, g, k, v, mask)
        add_block(rs, rs, q, g, k, a, f, dq_ref, dk_ref, dv_ref)
        return carry

    lax.fori_loop(0, rows // BLOCK, diagonal, 0)
    for b in range(1, rows // BLOCK):
        query_rows, key_row = pair_limits(lengths_ref, start + b * BLOCK, start, b * BLOCK)
        query_rows = jnp.minimum(query_rows, BLOCK)
        sweep(
            q_ref, g_ref, k_ref, v_ref, dq_ref, dk_ref, dv_ref, query_rows, key_row,
            q0=b * BLOCK, nk=b,
        )


def next_kernel(lengths_ref, qgn_ref, kv_ref, dk_in, dv_in, dqn_ref, dk_ref, dv_ref):
    rows = qgn_ref.shape[1]
    me = lax.axis_index("seq")
    dqn_ref[...] = jnp.zeros_like(dqn_ref)
    dk_ref[...] = dk_in[...]
    dv_ref[...] = dv_in[...]
    limits = pair_limits(lengths_ref, (me + 1) * rows, me * rows, rows)
    sweep(
        qgn_ref.at[0], qgn_ref.at[1], kv_ref.at[0], kv_ref.at[1], dqn_ref, dk_ref, dv_ref, *limits
    )


def far_kernel(
    lengths_ref, qg_ref, qgn_ref, kv_ref, dq_in, dqn_in, dk_own, dv_own,
    keep_ref, send_ref, dq_same, dq_cross, dkv_same, dkv_cross,
    dq_ref, dqn_ref, dk_ref, dv_ref,
):
    rows, width = dq_in.shape
    me = lax.axis_index("seq")
    dq_ref[...] = dq_in[...]
    dqn_ref[...] = dqn_in[...]
    dk_ref[...] = jnp.zeros_like(dk_ref)
    dv_ref[...] = jnp.zeros_like(dv_ref)
    k_ref, v_ref = kv_ref.at[0], kv_ref.at[1]
    key_start = (me - 2) * rows
    near = pair_limits(lengths_ref, me * rows, key_start, rows)
    sweep(qg_ref.at[0], qg_ref.at[1], k_ref, v_ref, dq_ref, dk_ref, dv_ref, *near)
    far = pair_limits(lengths_ref, (me + 1) * rows, key_start, rows)
    sweep(qgn_ref.at[0], qgn_ref.at[1], k_ref, v_ref, dqn_ref, dk_ref, dv_ref, *far)

    norm = MAXLEN**-0.5
    inner = 0.5 * norm * width**-0.5
    half = dq_same.shape[0]
    block = half // 2
    head = lax.axis_index("head")
    high, low = head // 2, head % 2
    for bit, dq_out, dkv_out in ((high, dq_same, dkv_same), (1 - high, dq_cross, dkv_cross)):
        src = pl.ds(pl.multiple_of(bit * half, half), half)
        dq_out[...] = (dqn_ref[src, :] * inner).astype(BF16)
        dkv_out[0] = (dk_ref[src, :] * inner).astype(BF16)
        dkv_out[1] = (dv_ref[src, :] * norm).astype(BF16)
    for bit, out_ref in ((low, keep_ref), (1 - low, send_ref)):
        for top in range(2):
            src = pl.ds(pl.multiple_of((2 * top + bit) * block, block), block)
            dst = pl.ds(top * block, block)
            own = (dq_ref[src, :] * inner, dk_own[src, :] * inner, dv_own[src, :] * norm)
            for c, part in enumerate(own):
                out_ref[c, dst, :] = part.astype(BF16)


def project(grads, weights):
    return lax.dot_general(
        jnp.concatenate(grads, axis=1), jnp.concatenate(weights, axis=1),
        (((1,), (1,)), ((), ())), preferred_element_type=F32,
    )


def local_kernel(keep_ref, got_ref, w_ref, w1_ref, mine_ref, send_ref):
    block = mine_ref.shape[0]
    high = lax.axis_index("head") // 2
    weights = [ref[c] for ref in (w_ref, w1_ref) for c in range(3)]
    for bit, out_ref in ((1 - high, send_ref), (high, mine_ref)):
        src = pl.ds(pl.multiple_of(bit * block, block), block)
        grads = [ref[c, src, :] for ref in (keep_ref, got_ref) for c in range(3)]
        out_ref[...] = project(grads, weights).astype(out_ref.dtype)


def split_kernel(dq_same, dkv_same, dq_cross, dkv_cross, keep_ref, send_ref):
    block = keep_ref.shape[2]
    low = lax.axis_index("head") % 2
    for bit, out_ref in ((1 - low, send_ref), (low, keep_ref)):
        src = pl.ds(pl.multiple_of(bit * block, block), block)
        for n, (dq, dkv) in enumerate(((dq_same, dkv_same), (dq_cross, dkv_cross))):
            out_ref[n, 0] = dq[src, :]
            out_ref[n, 1] = dkv[0, src, :]
            out_ref[n, 2] = dkv[1, src, :]


def final_kernel(keep_ref, got_ref, mine_ref, arrived_ref, w_ref, w1_ref, w2_ref, w3_ref, out_ref):
    grads, weights = [], []
    for half_ref, pair in ((keep_ref, (w_ref, w2_ref)), (got_ref, (w1_ref, w3_ref))):
        for n, weight in enumerate(pair):
            grads += [half_ref[n, c] for c in range(3)]
            weights += [weight[c] for c in range(3)]
    out_ref[...] = project(grads, weights) + mine_ref[...] + arrived_ref[...].astype(F32)


def call(body, outs, args, flops, scratch=(), lengths=True, space=VMEM, limit=24):
    specs = [SMEM if lengths and n == 0 else space for n in range(len(args))]
    moved = sum(math.prod(a.shape) * a.dtype.itemsize for a in (*args, *outs))
    return pl.pallas_call(
        body,
        out_shape=outs,
        in_specs=specs,
        out_specs=tuple(VMEM for _ in outs),
        scratch_shapes=scratch,
        compiler_params=pltpu.CompilerParams(vmem_limit_bytes=limit * 2**20),
        cost_estimate=pl.CostEstimate(flops=flops, bytes_accessed=moved, transcendentals=0),
    )(*args)


def shards(queries, keys, values, out_grad, lengths, w_proj):
    rows, width = queries.shape
    model = w_proj.shape[1]
    heads = lax.axis_size("head")
    block = rows // heads
    like = jax.ShapeDtypeStruct
    wide = like((rows, width), F32)
    pair = like((2, rows, width), BF16)
    pair_flops = 10 * rows * rows * width

    query_grad, key_value = call(
        pack_kernel, (pair, pair), tuple(pltpu.with_memory_space_constraint(x, pltpu.HBM) for x in (queries, out_grad, keys, values)), 1000,
        scratch=[pltpu.SemaphoreType.DMA((4,))], lengths=False,
        space=pl.BlockSpec(memory_space=pltpu.HBM),
    )
    query_grad_got = shift(query_grad, -1)
    key_value_got = shift(key_value, 2)
    w1, w2, w3 = (shift(w_proj, 0, flip) for flip in (1, 2, 3))

    dq, dk, dv = call(own_kernel, (wide, wide, wide), (lengths, query_grad, key_value), pair_flops)
    dqn, dk, dv = call(
        next_kernel, (wide, wide, wide),
        (lengths, query_grad_got, key_value, dk, dv), pair_flops,
    )
    keep, send, dq_same, dq_cross, dkv_same, dkv_cross = call(
        far_kernel,
        (
            like((3, 2 * block, width), BF16), like((3, 2 * block, width), BF16),
            like((2 * block, width), BF16), like((2 * block, width), BF16),
            like((2, 2 * block, width), BF16), like((2, 2 * block, width), BF16),
        ),
        (lengths, query_grad, query_grad_got, key_value_got, dq, dqn, dk, dv),
        pair_flops,
        scratch=[pltpu.VMEM((rows, width), F32)] * 4,
    )
    dkv_cross = shift(dkv_cross, -2, 2)
    dkv_same = shift(dkv_same, -2)
    dq_cross = shift(dq_cross, 1, 2)
    dq_same = shift(dq_same, 1)
    got = shift(send, 0, 1)
    mine, send = call(
        local_kernel, (like((block, model), F32), like((block, model), BF16)),
        (keep, got, w_proj, w1), 12 * block * width * model, lengths=False,
    )
    arrived = shift(send, 0, 2)

    quarter = like((2, 3, block, width), BF16)
    keep, send = call(
        split_kernel, (quarter, quarter), (dq_same, dkv_same, dq_cross, dkv_cross), 1000,
        lengths=False,
    )
    got = shift(send, 0, 1)
    (out,) = call(
        final_kernel, (like((block, model), F32),),
        (keep, got, mine, arrived, w_proj, w1, w2, w3), 24 * block * width * model, lengths=False,
    )
    return out


def solution(mesh):
    return jax.shard_map(
        shards,
        mesh=mesh,
        in_specs=(
            P("seq", "head"),
            P("seq", "head"),
            P("seq", "head"),
            P("seq", "head"),
            P(),
            P(None, None, "head"),
        ),
        out_specs=P(("seq", "head"), None),
        check_vma=False,
    )
```

```python
import math

import jax
import jax.numpy as jnp
from jax import lax
from jax.experimental import pallas as pl
from jax.experimental.pallas import tpu as pltpu
from jax.sharding import PartitionSpec as P


MAXLEN = 3072
F32 = jnp.float32
BF16 = jnp.bfloat16
VMEM = pl.BlockSpec(memory_space=pltpu.VMEM)
SMEM = pl.BlockSpec(memory_space=pltpu.SMEM)


def shift(value, by, flip=0):
    tiles, heads = lax.axis_size("seq"), lax.axis_size("head")
    pairs = [
        (t * heads + h, (t + by) * heads + (h ^ flip))
        for t in range(tiles)
        for h in range(heads)
        if 0 <= t + by < tiles
    ]
    return lax.ppermute(value, ("seq", "head"), pairs)


def user_bounds(lengths_ref, position):
    def step(u, carry):
        end, first, last = carry
        end = end + lengths_ref[u]
        past = end <= position
        return (
            end,
            jnp.where(past, end, first),
            jnp.where(past, last, jnp.minimum(last, end)),
        )

    zero = jnp.int32(0)
    _, first, last = lax.fori_loop(
        0, lengths_ref.shape[0], step, (zero, zero, jnp.int32(2**30))
    )
    return first, last


def pair_limits(lengths_ref, query_start, key_start, rows):
    first, last = user_bounds(lengths_ref, query_start)
    live = first <= key_start + rows - 1
    query_rows = jnp.where(live, jnp.minimum(last - query_start, rows), 0)
    key_row = jnp.maximum(first - key_start, 0)
    return query_rows, key_row


def scores(q, g, k, v, mask=None):
    nt = (((1,), (1,)), ((), ()))
    half = lax.dot_general(k, q, nt, preferred_element_type=F32) * (0.5 * q.shape[1] ** -0.5)
    da = lax.dot_general(v, g, nt, preferred_element_type=F32)
    t = jnp.tanh(half)
    p = half * t
    a = half + p
    f = (1.0 + t) * (1.0 + (half - p)) * da
    if mask is not None:
        a = jnp.where(mask, a, 0.0)
        f = jnp.where(mask, f, 0.0)
    return a.astype(BF16), f.astype(BF16)


def add_block(qs, ks, q, g, k, a, f, dq_ref, dk_ref, dv_ref):
    dv_ref[ks, :] += jnp.dot(a, g, preferred_element_type=F32)
    dk_ref[ks, :] += jnp.dot(f, q, preferred_element_type=F32)
    dq_ref[qs, :] += lax.dot_general(f, k, (((0,), (0,)), ((), ())), preferred_element_type=F32)


def sweep(qg_ref, kv_ref, dq_ref, dk_ref, dv_ref, query_rows, key_row, key_blocks):
    block, width = qg_ref.shape[1:]
    zero = jnp.zeros((), BF16)
    row = lax.broadcasted_iota(jnp.int32, (block, width), 0)
    everything = pl.ds(0, block)

    def key_block(kb, carry):
        off = pl.multiple_of(kb * block, block)
        ks = pl.ds(off, block)
        kept, kept_keys = row < query_rows, row + off >= key_row
        q = jnp.where(kept, qg_ref[0], zero)
        g = jnp.where(kept, qg_ref[1], zero)
        k = jnp.where(kept_keys, kv_ref[0, ks, :], zero)
        v = jnp.where(kept_keys, kv_ref[1, ks, :], zero)
        a, f = scores(q, g, k, v)
        add_block(everything, ks, q, g, k, a, f, dq_ref, dk_ref, dv_ref)
        return carry

    first = jnp.where(query_rows > 0, key_row // block, key_blocks)
    lax.fori_loop(first, key_blocks, key_block, 0)


def halves(ref):
    half = ref.shape[0] // 2
    return ref.at[pl.ds(0, half)], ref.at[pl.ds(half, half)]


def pack_kernel(q_hbm, g_hbm, k_hbm, v_hbm, qa_ref, qb_ref, kv_ref, sems):
    half = qa_ref.shape[1]
    copies = [
        pltpu.make_async_copy(k_hbm, kv_ref.at[0], sems.at[0]),
        pltpu.make_async_copy(v_hbm, kv_ref.at[1], sems.at[1]),
    ]
    for n, ref in enumerate((qa_ref, qb_ref)):
        for m, hbm in enumerate((q_hbm, g_hbm)):
            part = hbm.at[pl.ds(n * half, half)]
            copies.append(pltpu.make_async_copy(part, ref.at[m], sems.at[2 + 2 * n + m]))
    for copy in copies:
        copy.start()
    for copy in copies:
        copy.wait()


def own_kernel(lengths_ref, qa_ref, qb_ref, kv_ref, dq_ref, dk_ref, dv_ref):
    block = qa_ref.shape[1]
    strip = block // 2
    start = lax.axis_index("seq") * (2 * block)
    dq_ref[...] = jnp.zeros_like(dq_ref)
    dk_ref[...] = jnp.zeros_like(dk_ref)
    dv_ref[...] = jnp.zeros_like(dv_ref)

    for b, qg_ref in enumerate((qa_ref, qb_ref)):
        query = lax.broadcasted_iota(jnp.int32, (1, block), 1) + start + b * block

        def step(u, carry):
            end, first = carry
            end = end + lengths_ref[u]
            return end, jnp.where(end <= query, end, first)

        _, first = lax.fori_loop(
            0, lengths_ref.shape[0], step, (jnp.int32(0), jnp.zeros((1, block), jnp.int32))
        )
        for off in range(0, block, strip):
            ks, qs = pl.ds(b * block + off, strip), pl.ds(b * block + off, block - off)
            key = lax.broadcasted_iota(jnp.int32, (strip, block - off), 0) + start + b * block + off
            mask = (key <= query[:, off:]) & (key >= first[:, off:])
            q, g = qg_ref[0, off:, :], qg_ref[1, off:, :]
            k, v = kv_ref[0, ks, :], kv_ref[1, ks, :]
            a, f = scores(q, g, k, v, mask)
            add_block(qs, ks, q, g, k, a, f, dq_ref, dk_ref, dv_ref)

    query_rows, key_row = pair_limits(lengths_ref, start + block, start, block)
    sweep(qb_ref, kv_ref, halves(dq_ref)[1], dk_ref, dv_ref, query_rows, key_row, 1)


def next_kernel(lengths_ref, qan_ref, kv_ref, dk_in, dv_in, dqn_ref, dk_ref, dv_ref):
    rows = kv_ref.shape[1]
    me = lax.axis_index("seq")
    dqn_ref[...] = jnp.zeros_like(dqn_ref)
    dk_ref[...] = dk_in[...]
    dv_ref[...] = dv_in[...]
    query_rows, key_row = pair_limits(lengths_ref, (me + 1) * rows, me * rows, rows)
    sweep(qan_ref, kv_ref, dqn_ref, dk_ref, dv_ref, query_rows, key_row, 2)


def near_kernel(lengths_ref, qa_ref, qb_ref, kvn_ref, dq_in, dq_ref, dkn_ref, dvn_ref):
    half, rows = qa_ref.shape[1], kvn_ref.shape[1]
    me = lax.axis_index("seq")
    dq_ref[...] = dq_in[...]
    dkn_ref[...] = jnp.zeros_like(dkn_ref)
    dvn_ref[...] = jnp.zeros_like(dvn_ref)
    query_rows, key_row = pair_limits(lengths_ref, me * rows, (me - 2) * rows, rows)
    for n, (qg_ref, dq) in enumerate(zip((qa_ref, qb_ref), halves(dq_ref))):
        sweep(qg_ref, kvn_ref, dq, dkn_ref, dvn_ref, query_rows - n * half, key_row, 2)


def rest_kernel(
    lengths_ref, qan_ref, qbn_ref, kv_ref, kvn_ref,
    dq_ref, dqa_in, dk_in, dv_in, dkn_in, dvn_in,
    keep_ref, send_ref, dq_same, dq_cross, dkv_same, dkv_cross,
    dqa_ref, dqb_ref, dk_own, dv_own, dk_ref, dv_ref,
):
    width = dq_ref.shape[1]
    rows = kv_ref.shape[1]
    me = lax.axis_index("seq")
    dqa_ref[...] = dqa_in[...]
    dqb_ref[...] = jnp.zeros_like(dqb_ref)
    dk_own[...] = dk_in[...]
    dv_own[...] = dv_in[...]
    dk_ref[...] = dkn_in[...]
    dv_ref[...] = dvn_in[...]
    query_rows, key_row = pair_limits(lengths_ref, (me + 1) * rows, me * rows, rows)
    sweep(qbn_ref, kv_ref, dqb_ref, dk_own, dv_own, query_rows - rows // 2, key_row, 2)
    query_rows, key_row = pair_limits(lengths_ref, (me + 1) * rows, (me - 2) * rows, rows)
    sweep(qan_ref, kvn_ref, dqa_ref, dk_ref, dv_ref, query_rows, key_row, 2)
    sweep(qbn_ref, kvn_ref, dqb_ref, dk_ref, dv_ref, query_rows - rows // 2, key_row, 2)

    norm = MAXLEN**-0.5
    inner = 0.5 * norm * width**-0.5
    half = dq_same.shape[0]
    block = half // 2
    head = lax.axis_index("head")
    high, low = head // 2, head % 2
    for bit, dq_out, dkv_out in ((high, dq_same, dkv_same), (1 - high, dq_cross, dkv_cross)):
        src = pl.ds(pl.multiple_of(bit * half, half), half)
        dq_out[...] = (jnp.where(bit == 0, dqa_ref[...], dqb_ref[...]) * inner).astype(BF16)
        dkv_out[0] = (dk_ref[src, :] * inner).astype(BF16)
        dkv_out[1] = (dv_ref[src, :] * norm).astype(BF16)
    for bit, out_ref in ((low, keep_ref), (1 - low, send_ref)):
        for top in range(2):
            src = pl.ds(pl.multiple_of((2 * top + bit) * block, block), block)
            dst = pl.ds(top * block, block)
            own = (dq_ref[src, :] * inner, dk_own[src, :] * inner, dv_own[src, :] * norm)
            for c, part in enumerate(own):
                out_ref[c, dst, :] = part.astype(BF16)


def project(grads, weights):
    return lax.dot_general(
        jnp.concatenate(grads, axis=1), jnp.concatenate(weights, axis=1),
        (((1,), (1,)), ((), ())), preferred_element_type=F32,
    )


def local_kernel(keep_ref, got_ref, w_ref, w1_ref, mine_ref, send_ref):
    block = mine_ref.shape[0]
    high = lax.axis_index("head") // 2
    weights = [ref[c] for ref in (w_ref, w1_ref) for c in range(3)]
    for bit, out_ref in ((1 - high, send_ref), (high, mine_ref)):
        src = pl.ds(pl.multiple_of(bit * block, block), block)
        grads = [ref[c, src, :] for ref in (keep_ref, got_ref) for c in range(3)]
        out_ref[...] = project(grads, weights).astype(out_ref.dtype)


def split_kernel(dq_same, dkv_same, dq_cross, dkv_cross, keep_ref, send_ref):
    block = keep_ref.shape[2]
    low = lax.axis_index("head") % 2
    for bit, out_ref in ((1 - low, send_ref), (low, keep_ref)):
        src = pl.ds(pl.multiple_of(bit * block, block), block)
        for n, (dq, dkv) in enumerate(((dq_same, dkv_same), (dq_cross, dkv_cross))):
            out_ref[n, 0] = dq[src, :]
            out_ref[n, 1] = dkv[0, src, :]
            out_ref[n, 2] = dkv[1, src, :]


def final_kernel(keep_ref, got_ref, mine_ref, arrived_ref, w_ref, w1_ref, w2_ref, w3_ref, out_ref):
    grads, weights = [], []
    for half_ref, pair in ((keep_ref, (w_ref, w2_ref)), (got_ref, (w1_ref, w3_ref))):
        for n, weight in enumerate(pair):
            grads += [half_ref[n, c] for c in range(3)]
            weights += [weight[c] for c in range(3)]
    out_ref[...] = project(grads, weights) + mine_ref[...] + arrived_ref[...].astype(F32)


def call(body, outs, args, flops, scratch=(), lengths=True, space=VMEM, limit=24):
    specs = [SMEM if lengths and n == 0 else space for n in range(len(args))]
    moved = sum(math.prod(a.shape) * a.dtype.itemsize for a in (*args, *outs))
    return pl.pallas_call(
        body,
        out_shape=outs,
        in_specs=specs,
        out_specs=tuple(VMEM for _ in outs),
        scratch_shapes=scratch,
        compiler_params=pltpu.CompilerParams(vmem_limit_bytes=limit * 2**20),
        cost_estimate=pl.CostEstimate(flops=flops, bytes_accessed=moved, transcendentals=0),
    )(*args)


def shards(queries, keys, values, out_grad, lengths, w_proj):
    rows, width = queries.shape
    model = w_proj.shape[1]
    heads = lax.axis_size("head")
    block = rows // heads
    like = jax.ShapeDtypeStruct
    wide = like((rows, width), F32)
    pair_flops = 10 * rows * rows * width

    half = like((2, rows // 2, width), BF16)
    half_wide = like((rows // 2, width), F32)
    inputs = (queries, out_grad, keys, values)
    qa, qb, kv = call(
        pack_kernel, (half, half, like((2, rows, width), BF16)),
        tuple(pltpu.with_memory_space_constraint(x, pltpu.HBM) for x in inputs), 1000,
        scratch=[pltpu.SemaphoreType.DMA((6,))], lengths=False,
        space=pl.BlockSpec(memory_space=pltpu.HBM),
    )
    kvn = shift(kv, 2)
    qan = shift(qa, -1)
    qbn = shift(qb, -1)
    w2 = shift(w_proj, 0, 2)

    dq, dk, dv = call(own_kernel, (wide, wide, wide), (lengths, qa, qb, kv), pair_flops)
    dqn, dk, dv = call(next_kernel, (half_wide, wide, wide), (lengths, qan, kv, dk, dv), pair_flops)
    dq, dkn, dvn = call(near_kernel, (wide, wide, wide), (lengths, qa, qb, kvn, dq), pair_flops)
    keep, send, dq_same, dq_cross, dkv_same, dkv_cross = call(
        rest_kernel,
        (
            like((3, 2 * block, width), BF16), like((3, 2 * block, width), BF16),
            like((2 * block, width), BF16), like((2 * block, width), BF16),
            like((2, 2 * block, width), BF16), like((2, 2 * block, width), BF16),
        ),
        (lengths, qan, qbn, kv, kvn, dq, dqn, dk, dv, dkn, dvn), pair_flops,
        scratch=[pltpu.VMEM((rows // 2, width), F32)] * 2 + [pltpu.VMEM((rows, width), F32)] * 4,
    )
    w1, w3 = shift(w_proj, 0, 1), shift(w2, 0, 1)
    dkv_cross = shift(dkv_cross, -2, 2)
    dkv_same = shift(dkv_same, -2)
    dq_cross = shift(dq_cross, 1, 2)
    dq_same = shift(dq_same, 1)
    got = shift(send, 0, 1)
    mine, send = call(
        local_kernel, (like((block, model), F32), like((block, model), BF16)),
        (keep, got, w_proj, w1), 12 * block * width * model, lengths=False,
    )
    arrived = shift(send, 0, 2)

    quarter = like((2, 3, block, width), BF16)
    keep, send = call(
        split_kernel, (quarter, quarter), (dq_same, dkv_same, dq_cross, dkv_cross), 1000,
        lengths=False,
    )
    got = shift(send, 0, 1)
    (out,) = call(
        final_kernel, (like((block, model), F32),),
        (keep, got, mine, arrived, w_proj, w1, w2, w3), 24 * block * width * model, lengths=False,
    )
    return out


def solution(mesh):
    return jax.shard_map(
        shards,
        mesh=mesh,
        in_specs=(
            P("seq", "head"),
            P("seq", "head"),
            P("seq", "head"),
            P("seq", "head"),
            P(),
            P(None, None, "head"),
        ),
        out_specs=P(("seq", "head"), None),
        check_vma=False,
    )
```

```python
import math

import jax
import jax.numpy as jnp
from jax import lax
from jax.experimental import pallas as pl
from jax.experimental.pallas import tpu as pltpu
from jax.sharding import PartitionSpec as P


MAXLEN = 3072
F32 = jnp.float32
BF16 = jnp.bfloat16
VMEM = pl.BlockSpec(memory_space=pltpu.VMEM)
SMEM = pl.BlockSpec(memory_space=pltpu.SMEM)


def shift(value, by, flip=0):
    tiles, heads = lax.axis_size("seq"), lax.axis_size("head")
    pairs = [
        (t * heads + h, (t + by) * heads + (h ^ flip))
        for t in range(tiles)
        for h in range(heads)
        if 0 <= t + by < tiles
    ]
    return lax.ppermute(value, ("seq", "head"), pairs)


def user_bounds(lengths_ref, position):
    def step(u, carry):
        end, first, last = carry
        end = end + lengths_ref[u]
        past = end <= position
        return (
            end,
            jnp.where(past, end, first),
            jnp.where(past, last, jnp.minimum(last, end)),
        )

    zero = jnp.int32(0)
    _, first, last = lax.fori_loop(
        0, lengths_ref.shape[0], step, (zero, zero, jnp.int32(2**30))
    )
    return first, last


def pair_limits(lengths_ref, query_start, key_start, rows):
    first, last = user_bounds(lengths_ref, query_start)
    live = first <= key_start + rows - 1
    query_rows = jnp.where(live, jnp.minimum(last - query_start, rows), 0)
    key_row = jnp.maximum(first - key_start, 0)
    return query_rows, key_row


def scores(q, g, k, v, mask=None):
    nt = (((1,), (1,)), ((), ()))
    half = lax.dot_general(k, q, nt, preferred_element_type=F32) * (0.5 * q.shape[1] ** -0.5)
    da = lax.dot_general(v, g, nt, preferred_element_type=F32)
    gate = 1.0 + jnp.tanh(half)
    if mask is not None:
        gate = jnp.where(mask, gate, 0.0)
    a = half * gate
    f = (gate + a * (2.0 - gate)) * da
    return a.astype(BF16), f.astype(BF16)


def add_block(qs, ks, q, g, k, a, f, dq_ref, dk_ref, dv_ref):
    dv_ref[ks, :] += jnp.dot(a, g, preferred_element_type=F32)
    dk_ref[ks, :] += jnp.dot(f, q, preferred_element_type=F32)
    dq_ref[qs, :] += lax.dot_general(f, k, (((0,), (0,)), ((), ())), preferred_element_type=F32)


def copy_rows(out_ref, ref, start, low, high):
    block, width = out_ref.shape[1:]
    src = pl.ds(start, block)
    inside = (low <= 0) & (high >= block)

    @pl.when(inside)
    def _():
        for n in range(2):
            out_ref[n] = ref[n, src, :]

    @pl.when(jnp.logical_not(inside))
    def _():
        row = lax.broadcasted_iota(jnp.int32, (block, width), 0)
        kept = (row >= low) & (row < high)
        for n in range(2):
            out_ref[n] = jnp.where(kept, ref[n, src, :], jnp.zeros((), BF16))


def sweep(
    qg_ref, kv_ref, dq_ref, dk_ref, dv_ref, query_rows, key_row, key_blocks, qm_ref, km_ref
):
    block = qg_ref.shape[1]
    everything = pl.ds(0, block)

    @pl.when(query_rows > 0)
    def _():
        copy_rows(qm_ref, qg_ref, 0, 0, query_rows)

        def key_block(kb, carry):
            off = pl.multiple_of(kb * block, block)
            ks = pl.ds(off, block)
            copy_rows(km_ref, kv_ref, off, key_row - off, block)
            q, g, k, v = qm_ref[0], qm_ref[1], km_ref[0], km_ref[1]
            a, f = scores(q, g, k, v)
            add_block(everything, ks, q, g, k, a, f, dq_ref, dk_ref, dv_ref)
            return carry

        lax.fori_loop(key_row // block, key_blocks, key_block, 0)


def halves(ref):
    half = ref.shape[0] // 2
    return ref.at[pl.ds(0, half)], ref.at[pl.ds(half, half)]


def pack_kernel(q_hbm, g_hbm, k_hbm, v_hbm, qa_ref, qb_ref, kv_ref, sems):
    half = qa_ref.shape[1]
    copies = [
        pltpu.make_async_copy(k_hbm, kv_ref.at[0], sems.at[0]),
        pltpu.make_async_copy(v_hbm, kv_ref.at[1], sems.at[1]),
    ]
    for n, ref in enumerate((qa_ref, qb_ref)):
        for m, hbm in enumerate((q_hbm, g_hbm)):
            part = hbm.at[pl.ds(n * half, half)]
            copies.append(pltpu.make_async_copy(part, ref.at[m], sems.at[2 + 2 * n + m]))
    for copy in copies:
        copy.start()
    for copy in copies:
        copy.wait()


def own_kernel(lengths_ref, qa_ref, qb_ref, kv_ref, dq_ref, dk_ref, dv_ref, *masked):
    block = qa_ref.shape[1]
    strip = block // 2
    start = lax.axis_index("seq") * (2 * block)
    dq_ref[...] = jnp.zeros_like(dq_ref)
    dk_ref[...] = jnp.zeros_like(dk_ref)
    dv_ref[...] = jnp.zeros_like(dv_ref)

    for b, qg_ref in enumerate((qa_ref, qb_ref)):
        query = lax.broadcasted_iota(jnp.int32, (1, block), 1) + start + b * block

        def step(u, carry):
            end, first = carry
            end = end + lengths_ref[u]
            return end, jnp.where(end <= query, end, first)

        _, first = lax.fori_loop(
            0, lengths_ref.shape[0], step, (jnp.int32(0), jnp.zeros((1, block), jnp.int32))
        )
        for off in range(0, block, strip):
            ks, qs = pl.ds(b * block + off, strip), pl.ds(b * block + off, block - off)
            key = lax.broadcasted_iota(jnp.int32, (strip, block - off), 0) + start + b * block + off
            mask = (key <= query[:, off:]) & (key >= first[:, off:])
            q, g = qg_ref[0, off:, :], qg_ref[1, off:, :]
            k, v = kv_ref[0, ks, :], kv_ref[1, ks, :]
            a, f = scores(q, g, k, v, mask)
            add_block(qs, ks, q, g, k, a, f, dq_ref, dk_ref, dv_ref)

    query_rows, key_row = pair_limits(lengths_ref, start + block, start, block)
    sweep(qb_ref, kv_ref, halves(dq_ref)[1], dk_ref, dv_ref, query_rows, key_row, 1, *masked)


def next_kernel(
    lengths_ref, qan_ref, kv_ref, dk_in, dv_in, dqn_ref, dk_ref, dv_ref, *masked
):
    rows = kv_ref.shape[1]
    me = lax.axis_index("seq")
    dqn_ref[...] = jnp.zeros_like(dqn_ref)
    query_rows, key_row = pair_limits(lengths_ref, (me + 1) * rows, me * rows, rows)
    sweep(qan_ref, kv_ref, dqn_ref, dk_ref, dv_ref, query_rows, key_row, 2, *masked)


def near_kernel(
    lengths_ref, qa_ref, qb_ref, kvn_ref, dq_in, dq_ref, dkn_ref, dvn_ref, *masked
):
    half, rows = qa_ref.shape[1], kvn_ref.shape[1]
    me = lax.axis_index("seq")
    dkn_ref[...] = jnp.zeros_like(dkn_ref)
    dvn_ref[...] = jnp.zeros_like(dvn_ref)
    query_rows, key_row = pair_limits(lengths_ref, me * rows, (me - 2) * rows, rows)
    for n, (qg_ref, dq) in enumerate(zip((qa_ref, qb_ref), halves(dq_ref))):
        sweep(qg_ref, kvn_ref, dq, dkn_ref, dvn_ref, query_rows - n * half, key_row, 2, *masked)


def rest_kernel(
    lengths_ref, qan_ref, qbn_ref, kv_ref, kvn_ref,
    dq_ref, dqa_in, dk_in, dv_in, dkn_in, dvn_in,
    keep_ref, send_ref, dq_same, dq_cross, dkv_same, dkv_cross,
    dqa_ref, dk_own, dv_own, dk_ref, dv_ref,
    dqb_ref, *masked,
):
    width = dq_ref.shape[1]
    rows = kv_ref.shape[1]
    me = lax.axis_index("seq")
    dqb_ref[...] = jnp.zeros_like(dqb_ref)
    query_rows, key_row = pair_limits(lengths_ref, (me + 1) * rows, me * rows, rows)
    tail_rows = query_rows - rows // 2
    sweep(qbn_ref, kv_ref, dqb_ref, dk_own, dv_own, tail_rows, key_row, 2, *masked)
    query_rows, key_row = pair_limits(lengths_ref, (me + 1) * rows, (me - 2) * rows, rows)
    tail_rows = query_rows - rows // 2
    sweep(qan_ref, kvn_ref, dqa_ref, dk_ref, dv_ref, query_rows, key_row, 2, *masked)
    sweep(qbn_ref, kvn_ref, dqb_ref, dk_ref, dv_ref, tail_rows, key_row, 2, *masked)

    norm = MAXLEN**-0.5
    inner = 0.5 * norm * width**-0.5
    half = dq_same.shape[0]
    block = half // 2
    head = lax.axis_index("head")
    high, low = head // 2, head % 2
    for bit, dq_out, dkv_out in ((high, dq_same, dkv_same), (1 - high, dq_cross, dkv_cross)):
        src = pl.ds(pl.multiple_of(bit * half, half), half)
        dq_out[...] = (jnp.where(bit == 0, dqa_ref[...], dqb_ref[...]) * inner).astype(BF16)
        dkv_out[0] = (dk_ref[src, :] * inner).astype(BF16)
        dkv_out[1] = (dv_ref[src, :] * norm).astype(BF16)
    for bit, out_ref in ((low, keep_ref), (1 - low, send_ref)):
        for top in range(2):
            src = pl.ds(pl.multiple_of((2 * top + bit) * block, block), block)
            dst = pl.ds(top * block, block)
            own = (dq_ref[src, :] * inner, dk_own[src, :] * inner, dv_own[src, :] * norm)
            for c, part in enumerate(own):
                out_ref[c, dst, :] = part.astype(BF16)


def project(grads, weights):
    return lax.dot_general(
        jnp.concatenate(grads, axis=1), jnp.concatenate(weights, axis=1),
        (((1,), (1,)), ((), ())), preferred_element_type=F32,
    )


def local_kernel(keep_ref, got_ref, w_ref, w1_ref, mine_ref, send_ref):
    block = mine_ref.shape[0]
    high = lax.axis_index("head") // 2
    weights = [ref[c] for ref in (w_ref, w1_ref) for c in range(3)]
    for bit, out_ref in ((1 - high, send_ref), (high, mine_ref)):
        src = pl.ds(pl.multiple_of(bit * block, block), block)
        grads = [ref[c, src, :] for ref in (keep_ref, got_ref) for c in range(3)]
        out_ref[...] = project(grads, weights).astype(out_ref.dtype)


def split_kernel(dq_same, dkv_same, dq_cross, dkv_cross, keep_ref, send_ref):
    block = keep_ref.shape[2]
    low = lax.axis_index("head") % 2
    for bit, out_ref in ((1 - low, send_ref), (low, keep_ref)):
        src = pl.ds(pl.multiple_of(bit * block, block), block)
        for n, (dq, dkv) in enumerate(((dq_same, dkv_same), (dq_cross, dkv_cross))):
            out_ref[n, 0] = dq[src, :]
            out_ref[n, 1] = dkv[0, src, :]
            out_ref[n, 2] = dkv[1, src, :]


def final_kernel(keep_ref, got_ref, mine_ref, arrived_ref, w_ref, w1_ref, w2_ref, w3_ref, out_ref):
    grads, weights = [], []
    for half_ref, pair in ((keep_ref, (w_ref, w2_ref)), (got_ref, (w1_ref, w3_ref))):
        for n, weight in enumerate(pair):
            grads += [half_ref[n, c] for c in range(3)]
            weights += [weight[c] for c in range(3)]
    out_ref[...] = project(grads, weights) + mine_ref[...] + arrived_ref[...].astype(F32)


def call(body, outs, args, flops, scratch=(), lengths=True, space=VMEM, aliases=()):
    specs = [SMEM if lengths and n == 0 else space for n in range(len(args))]
    moved = sum(math.prod(a.shape) * a.dtype.itemsize for a in (*args, *outs))
    return pl.pallas_call(
        body,
        out_shape=outs,
        in_specs=specs,
        out_specs=tuple(VMEM for _ in outs),
        scratch_shapes=scratch,
        input_output_aliases=dict(aliases),
        compiler_params=pltpu.CompilerParams(vmem_limit_bytes=24 * 2**20),
        cost_estimate=pl.CostEstimate(flops=flops, bytes_accessed=moved, transcendentals=0),
    )(*args)


def shards(queries, keys, values, out_grad, lengths, w_proj):
    rows, width = queries.shape
    model = w_proj.shape[1]
    heads = lax.axis_size("head")
    block = rows // heads
    like = jax.ShapeDtypeStruct
    wide = like((rows, width), F32)
    pair_flops = 10 * rows * rows * width

    half = like((2, rows // 2, width), BF16)
    half_wide = like((rows // 2, width), F32)
    inputs = (queries, out_grad, keys, values)
    qa, qb, kv = call(
        pack_kernel, (half, half, like((2, rows, width), BF16)),
        tuple(pltpu.with_memory_space_constraint(x, pltpu.HBM) for x in inputs), 1000,
        scratch=[pltpu.SemaphoreType.DMA((6,))], lengths=False,
        space=pl.BlockSpec(memory_space=pltpu.HBM),
    )
    kvn = shift(kv, 2)
    qan = shift(qa, -1)
    qbn = shift(qb, -1)
    w2 = shift(w_proj, 0, 2)

    masked = [pltpu.VMEM((2, rows // 2, width), BF16)] * 2
    dq, dk, dv = call(
        own_kernel, (wide, wide, wide), (lengths, qa, qb, kv), pair_flops, scratch=masked
    )
    dqn, dk, dv = call(
        next_kernel, (half_wide, wide, wide), (lengths, qan, kv, dk, dv), pair_flops,
        scratch=masked, aliases=((3, 1), (4, 2)),
    )
    dq, dkn, dvn = call(
        near_kernel, (wide, wide, wide), (lengths, qa, qb, kvn, dq), pair_flops,
        scratch=masked, aliases=((4, 0),),
    )
    keep, send, dq_same, dq_cross, dkv_same, dkv_cross, *_ = call(
        rest_kernel,
        (
            like((3, 2 * block, width), BF16), like((3, 2 * block, width), BF16),
            like((2 * block, width), BF16), like((2 * block, width), BF16),
            like((2, 2 * block, width), BF16), like((2, 2 * block, width), BF16),
            half_wide, wide, wide, wide, wide,
        ),
        (lengths, qan, qbn, kv, kvn, dq, dqn, dk, dv, dkn, dvn), pair_flops,
        scratch=[pltpu.VMEM((rows // 2, width), F32), *masked],
        aliases=((6, 6), (7, 7), (8, 8), (9, 9), (10, 10)),
    )
    w1, w3 = shift(w_proj, 0, 1), shift(w2, 0, 1)
    dkv_cross = shift(dkv_cross, -2, 2)
    dkv_same = shift(dkv_same, -2)
    dq_cross = shift(dq_cross, 1, 2)
    dq_same = shift(dq_same, 1)
    got = shift(send, 0, 1)
    mine, send = call(
        local_kernel, (like((block, model), F32), like((block, model), BF16)),
        (keep, got, w_proj, w1), 12 * block * width * model, lengths=False,
    )
    arrived = shift(send, 0, 2)

    quarter = like((2, 3, block, width), BF16)
    keep, send = call(
        split_kernel, (quarter, quarter), (dq_same, dkv_same, dq_cross, dkv_cross), 1000,
        lengths=False,
    )
    got = shift(send, 0, 1)
    (out,) = call(
        final_kernel, (like((block, model), F32),),
        (keep, got, mine, arrived, w_proj, w1, w2, w3), 24 * block * width * model, lengths=False,
    )
    return out


def solution(mesh):
    return jax.shard_map(
        shards,
        mesh=mesh,
        in_specs=(
            P("seq", "head"),
            P("seq", "head"),
            P("seq", "head"),
            P("seq", "head"),
            P(),
            P(None, None, "head"),
        ),
        out_specs=P(("seq", "head"), None),
        check_vma=False,
    )
```

```python
import math

import jax
import jax.numpy as jnp
from jax import lax
from jax.experimental import pallas as pl
from jax.experimental.pallas import tpu as pltpu
from jax.sharding import PartitionSpec as P


MAXLEN = 3072
F32 = jnp.float32
BF16 = jnp.bfloat16
VMEM = pl.BlockSpec(memory_space=pltpu.VMEM)
SMEM = pl.BlockSpec(memory_space=pltpu.SMEM)


def shift(value, by, flip=0):
    tiles, heads = lax.axis_size("seq"), lax.axis_size("head")
    pairs = [
        (t * heads + h, (t + by) * heads + (h ^ flip))
        for t in range(tiles)
        for h in range(heads)
        if 0 <= t + by < tiles
    ]
    return lax.ppermute(value, ("seq", "head"), pairs)


def user_bounds(lengths_ref, position):
    def step(u, carry):
        end, first, last = carry
        end = end + lengths_ref[u]
        past = end <= position
        return (
            end,
            jnp.where(past, end, first),
            jnp.where(past, last, jnp.minimum(last, end)),
        )

    zero = jnp.int32(0)
    _, first, last = lax.fori_loop(
        0, lengths_ref.shape[0], step, (zero, zero, jnp.int32(2**30))
    )
    return first, last


def pair_limits(lengths_ref, query_start, key_start, rows):
    first, last = user_bounds(lengths_ref, query_start)
    live = first <= key_start + rows - 1
    query_rows = jnp.where(live, jnp.minimum(last - query_start, rows), 0)
    key_row = jnp.maximum(first - key_start, 0)
    return query_rows, key_row


def scores(q, g, k, v, mask=None):
    nt = (((1,), (1,)), ((), ()))
    half = lax.dot_general(k, q, nt, preferred_element_type=F32) * (0.5 * q.shape[1] ** -0.5)
    da = lax.dot_general(v, g, nt, preferred_element_type=F32)
    gate = 1.0 + jnp.tanh(half)
    if mask is not None:
        gate = jnp.where(mask, gate, 0.0)
    a = half * gate
    f = (gate + a * (2.0 - gate)) * da
    return a.astype(BF16), f.astype(BF16)


def add_block(qs, ks, q, g, k, a, f, dq_ref, dk_ref, dv_ref):
    dv_ref[ks, :] += jnp.dot(a, g, preferred_element_type=F32)
    dk_ref[ks, :] += jnp.dot(f, q, preferred_element_type=F32)
    dq_ref[qs, :] += lax.dot_general(f, k, (((0,), (0,)), ((), ())), preferred_element_type=F32)


def copy_rows(out_ref, ref, start, low, high):
    block, width = out_ref.shape[1:]
    src = pl.ds(start, block)
    inside = (low <= 0) & (high >= block)

    @pl.when(inside)
    def _():
        for n in range(2):
            out_ref[n] = ref[n, src, :]

    @pl.when(jnp.logical_not(inside))
    def _():
        row = lax.broadcasted_iota(jnp.int32, (block, width), 0)
        kept = (row >= low) & (row < high)
        for n in range(2):
            out_ref[n] = jnp.where(kept, ref[n, src, :], jnp.zeros((), BF16))


def sweep(
    qg_ref, kv_ref, dq_ref, dk_ref, dv_ref, query_rows, key_row, key_blocks, qm_ref, km_ref
):
    block = qg_ref.shape[1]
    everything = pl.ds(0, block)

    @pl.when(query_rows > 0)
    def _():
        copy_rows(qm_ref, qg_ref, 0, 0, query_rows)

        def key_block(kb, carry):
            off = pl.multiple_of(kb * block, block)
            ks = pl.ds(off, block)
            copy_rows(km_ref, kv_ref, off, key_row - off, block)
            q, g, k, v = qm_ref[0], qm_ref[1], km_ref[0], km_ref[1]
            a, f = scores(q, g, k, v)
            add_block(everything, ks, q, g, k, a, f, dq_ref, dk_ref, dv_ref)
            return carry

        lax.fori_loop(key_row // block, key_blocks, key_block, 0)


def halves(ref):
    half = ref.shape[0] // 2
    return ref.at[pl.ds(0, half)], ref.at[pl.ds(half, half)]


def pack_kernel(q_hbm, g_hbm, k_hbm, v_hbm, qa_ref, qb_ref, kv_ref, sems):
    half = qa_ref.shape[1]
    copies = [
        pltpu.make_async_copy(k_hbm, kv_ref.at[0], sems.at[0]),
        pltpu.make_async_copy(v_hbm, kv_ref.at[1], sems.at[1]),
    ]
    for n, ref in enumerate((qa_ref, qb_ref)):
        for m, hbm in enumerate((q_hbm, g_hbm)):
            part = hbm.at[pl.ds(n * half, half)]
            copies.append(pltpu.make_async_copy(part, ref.at[m], sems.at[2 + 2 * n + m]))
    for copy in copies:
        copy.start()
    for copy in copies:
        copy.wait()


def own_kernel(lengths_ref, qa_ref, qb_ref, kv_ref, dq_ref, dk_ref, dv_ref, *masked):
    block = qa_ref.shape[1]
    strip = block // 2
    start = lax.axis_index("seq") * (2 * block)
    dq_ref[...] = jnp.zeros_like(dq_ref)
    dk_ref[...] = jnp.zeros_like(dk_ref)
    dv_ref[...] = jnp.zeros_like(dv_ref)

    for b, qg_ref in enumerate((qa_ref, qb_ref)):
        query = lax.broadcasted_iota(jnp.int32, (1, block), 1) + start + b * block

        def step(u, carry):
            end, first = carry
            end = end + lengths_ref[u]
            return end, jnp.where(end <= query, end, first)

        _, first = lax.fori_loop(
            0, lengths_ref.shape[0], step, (jnp.int32(0), jnp.zeros((1, block), jnp.int32))
        )
        for off in range(0, block, strip):
            ks, qs = pl.ds(b * block + off, strip), pl.ds(b * block + off, block - off)
            key = lax.broadcasted_iota(jnp.int32, (strip, block - off), 0) + start + b * block + off
            mask = (key <= query[:, off:]) & (key >= first[:, off:])
            q, g = qg_ref[0, off:, :], qg_ref[1, off:, :]
            k, v = kv_ref[0, ks, :], kv_ref[1, ks, :]
            a, f = scores(q, g, k, v, mask)
            add_block(qs, ks, q, g, k, a, f, dq_ref, dk_ref, dv_ref)

    query_rows, key_row = pair_limits(lengths_ref, start + block, start, block)
    sweep(qb_ref, kv_ref, halves(dq_ref)[1], dk_ref, dv_ref, query_rows, key_row, 1, *masked)


def next_kernel(
    lengths_ref, qan_ref, kv_ref, dk_in, dv_in, dqn_ref, dk_ref, dv_ref, *masked
):
    rows = kv_ref.shape[1]
    me = lax.axis_index("seq")
    dqn_ref[...] = jnp.zeros_like(dqn_ref)
    query_rows, key_row = pair_limits(lengths_ref, (me + 1) * rows, me * rows, rows)
    sweep(qan_ref, kv_ref, dqn_ref, dk_ref, dv_ref, query_rows, key_row, 2, *masked)


def near_kernel(
    lengths_ref, qa_ref, qb_ref, kvn_ref, dq_in, dq_ref, dkn_ref, dvn_ref, *masked
):
    half, rows = qa_ref.shape[1], kvn_ref.shape[1]
    me = lax.axis_index("seq")
    dkn_ref[...] = jnp.zeros_like(dkn_ref)
    dvn_ref[...] = jnp.zeros_like(dvn_ref)
    query_rows, key_row = pair_limits(lengths_ref, me * rows, (me - 2) * rows, rows)
    for n, (qg_ref, dq) in enumerate(zip((qa_ref, qb_ref), halves(dq_ref))):
        sweep(qg_ref, kvn_ref, dq, dkn_ref, dvn_ref, query_rows - n * half, key_row, 2, *masked)


def rest_kernel(
    lengths_ref, qan_ref, qbn_ref, kv_ref, kvn_ref,
    dq_ref, dqa_in, dk_in, dv_in, dkn_in, dvn_in,
    dqn_out, dkv_same, dkv_cross,
    dqa_ref, dk_own, dv_own, dk_ref, dv_ref,
    dqb_ref, *masked,
):
    width = dq_ref.shape[1]
    rows = kv_ref.shape[1]
    me = lax.axis_index("seq")
    dqb_ref[...] = jnp.zeros_like(dqb_ref)
    query_rows, key_row = pair_limits(lengths_ref, (me + 1) * rows, me * rows, rows)
    tail_rows = query_rows - rows // 2
    sweep(qbn_ref, kv_ref, dqb_ref, dk_own, dv_own, tail_rows, key_row, 2, *masked)
    query_rows, key_row = pair_limits(lengths_ref, (me + 1) * rows, (me - 2) * rows, rows)
    tail_rows = query_rows - rows // 2
    sweep(qan_ref, kvn_ref, dqa_ref, dk_ref, dv_ref, query_rows, key_row, 2, *masked)
    sweep(qbn_ref, kvn_ref, dqb_ref, dk_ref, dv_ref, tail_rows, key_row, 2, *masked)

    norm = MAXLEN**-0.5
    inner = 0.5 * norm * width**-0.5
    half = rows // 2
    dqn_out[pl.ds(0, half), :] = (dqa_ref[...] * inner).astype(BF16)
    dqn_out[pl.ds(half, half), :] = (dqb_ref[...] * inner).astype(BF16)
    high = lax.axis_index("head") // 2
    for bit, dkv_out in ((high, dkv_same), (1 - high, dkv_cross)):
        src = pl.ds(pl.multiple_of(bit * half, half), half)
        dkv_out[0] = (dk_ref[src, :] * inner).astype(BF16)
        dkv_out[1] = (dv_ref[src, :] * norm).astype(BF16)


def join_kernel(dq_ref, dk_ref, dv_ref, dq_got, keep_ref, send_ref):
    width = dq_ref.shape[1]
    block = keep_ref.shape[1] // 2
    norm = MAXLEN**-0.5
    inner = 0.5 * norm * width**-0.5
    low = lax.axis_index("head") % 2
    for bit, out_ref in ((1 - low, send_ref), (low, keep_ref)):
        for top in range(2):
            src = pl.ds(pl.multiple_of((2 * top + bit) * block, block), block)
            dst = pl.ds(top * block, block)
            dq = dq_ref[src, :] * inner + dq_got[src, :].astype(F32)
            for c, part in enumerate((dq, dk_ref[src, :] * inner, dv_ref[src, :] * norm)):
                out_ref[c, dst, :] = part.astype(BF16)


def project(grads, weights):
    return lax.dot_general(
        jnp.concatenate(grads, axis=1), jnp.concatenate(weights, axis=1),
        (((1,), (1,)), ((), ())), preferred_element_type=F32,
    )


def local_kernel(keep_ref, got_ref, w_ref, w1_ref, mine_ref, send_ref):
    block = mine_ref.shape[0]
    high = lax.axis_index("head") // 2
    weights = [ref[c] for ref in (w_ref, w1_ref) for c in range(3)]
    for bit, out_ref in ((1 - high, send_ref), (high, mine_ref)):
        src = pl.ds(pl.multiple_of(bit * block, block), block)
        grads = [ref[c, src, :] for ref in (keep_ref, got_ref) for c in range(3)]
        out_ref[...] = project(grads, weights).astype(out_ref.dtype)


def split_kernel(dkv_same, dkv_cross, keep_ref, send_ref):
    block = keep_ref.shape[2]
    low = lax.axis_index("head") % 2
    for bit, out_ref in ((1 - low, send_ref), (low, keep_ref)):
        src = pl.ds(pl.multiple_of(bit * block, block), block)
        for n, dkv in enumerate((dkv_same, dkv_cross)):
            for c in range(2):
                out_ref[n, c] = dkv[c, src, :]


def returned(half_ref, weights):
    grads = [half_ref[n, c] for n in range(2) for c in range(2)]
    return project(grads, [weight[c] for weight in weights for c in (1, 2)])


def partial_kernel(keep_ref, mine_ref, w_ref, w2_ref, out_ref):
    out_ref[...] = mine_ref[...] + returned(keep_ref, (w_ref, w2_ref))


def final_kernel(got_ref, partial_ref, arrived_ref, w1_ref, w3_ref, out_ref):
    out_ref[...] = (
        partial_ref[...] + arrived_ref[...].astype(F32) + returned(got_ref, (w1_ref, w3_ref))
    )


def call(body, outs, args, flops, scratch=(), lengths=True, space=VMEM, aliases=()):
    specs = [SMEM if lengths and n == 0 else space for n in range(len(args))]
    moved = sum(math.prod(a.shape) * a.dtype.itemsize for a in (*args, *outs))
    return pl.pallas_call(
        body,
        out_shape=outs,
        in_specs=specs,
        out_specs=tuple(VMEM for _ in outs),
        scratch_shapes=scratch,
        input_output_aliases=dict(aliases),
        compiler_params=pltpu.CompilerParams(vmem_limit_bytes=24 * 2**20),
        cost_estimate=pl.CostEstimate(flops=flops, bytes_accessed=moved, transcendentals=0),
    )(*args)


def shards(queries, keys, values, out_grad, lengths, w_proj):
    rows, width = queries.shape
    model = w_proj.shape[1]
    heads = lax.axis_size("head")
    block = rows // heads
    like = jax.ShapeDtypeStruct
    wide = like((rows, width), F32)
    pair_flops = 10 * rows * rows * width

    half = like((2, rows // 2, width), BF16)
    half_wide = like((rows // 2, width), F32)
    inputs = (queries, out_grad, keys, values)
    qa, qb, kv = call(
        pack_kernel, (half, half, like((2, rows, width), BF16)),
        tuple(pltpu.with_memory_space_constraint(x, pltpu.HBM) for x in inputs), 1000,
        scratch=[pltpu.SemaphoreType.DMA((6,))], lengths=False,
        space=pl.BlockSpec(memory_space=pltpu.HBM),
    )
    kvn = shift(kv, 2)
    qan = shift(qa, -1)
    qbn = shift(qb, -1)
    w2 = shift(w_proj, 0, 2)

    masked = [pltpu.VMEM((2, rows // 2, width), BF16)] * 2
    dq, dk, dv = call(
        own_kernel, (wide, wide, wide), (lengths, qa, qb, kv), pair_flops, scratch=masked
    )
    dqn, dk, dv = call(
        next_kernel, (half_wide, wide, wide), (lengths, qan, kv, dk, dv), pair_flops,
        scratch=masked, aliases=((3, 1), (4, 2)),
    )
    dq, dkn, dvn = call(
        near_kernel, (wide, wide, wide), (lengths, qa, qb, kvn, dq), pair_flops,
        scratch=masked, aliases=((4, 0),),
    )
    dqn, dkv_same, dkv_cross, _, dk, dv, *_ = call(
        rest_kernel,
        (
            like((rows, width), BF16),
            like((2, 2 * block, width), BF16), like((2, 2 * block, width), BF16),
            half_wide, wide, wide, wide, wide,
        ),
        (lengths, qan, qbn, kv, kvn, dq, dqn, dk, dv, dkn, dvn), pair_flops,
        scratch=[pltpu.VMEM((rows // 2, width), F32), *masked],
        aliases=((6, 3), (7, 4), (8, 5), (9, 6), (10, 7)),
    )
    w1, w3 = shift(w_proj, 0, 1), shift(w2, 0, 1)
    dq_got = shift(dqn, 1)
    dkv_cross = shift(dkv_cross, -2, 2)
    dkv_same = shift(dkv_same, -2)

    packed = like((3, 2 * block, width), BF16)
    keep, send = call(join_kernel, (packed, packed), (dq, dk, dv, dq_got), 1000, lengths=False)
    got = shift(send, 0, 1)
    mine, send = call(
        local_kernel, (like((block, model), F32), like((block, model), BF16)),
        (keep, got, w_proj, w1), 12 * block * width * model, lengths=False,
    )
    arrived = shift(send, 0, 2)

    quarter = like((2, 2, block, width), BF16)
    keep, send = call(split_kernel, (quarter, quarter), (dkv_same, dkv_cross), 1000, lengths=False)
    got = shift(send, 0, 1)
    (mine,) = call(
        partial_kernel, (like((block, model), F32),), (keep, mine, w_proj, w2),
        8 * block * width * model, lengths=False,
    )
    (out,) = call(
        final_kernel, (like((block, model), F32),), (got, mine, arrived, w1, w3),
        8 * block * width * model, lengths=False,
    )
    return out


def solution(mesh):
    return jax.shard_map(
        shards,
        mesh=mesh,
        in_specs=(
            P("seq", "head"),
            P("seq", "head"),
            P("seq", "head"),
            P("seq", "head"),
            P(),
            P(None, None, "head"),
        ),
        out_specs=P(("seq", "head"), None),
        check_vma=False,
    )
```

```python
import math

import jax
import jax.numpy as jnp
from jax import lax
from jax.experimental import pallas as pl
from jax.experimental.pallas import tpu as pltpu
from jax.sharding import PartitionSpec as P


MAXLEN = 3072
F32 = jnp.float32
BF16 = jnp.bfloat16
VMEM = pl.BlockSpec(memory_space=pltpu.VMEM)
SMEM = pl.BlockSpec(memory_space=pltpu.SMEM)


def shift(value, by, flip=0):
    tiles, heads = lax.axis_size("seq"), lax.axis_size("head")
    pairs = [
        (t * heads + h, (t + by) * heads + (h ^ flip))
        for t in range(tiles)
        for h in range(heads)
        if 0 <= t + by < tiles
    ]
    return lax.ppermute(value, ("seq", "head"), pairs)


def user_bounds(lengths_ref, position):
    def step(u, carry):
        end, first, last = carry
        end = end + lengths_ref[u]
        past = end <= position
        return (
            end,
            jnp.where(past, end, first),
            jnp.where(past, last, jnp.minimum(last, end)),
        )

    zero = jnp.int32(0)
    _, first, last = lax.fori_loop(
        0, lengths_ref.shape[0], step, (zero, zero, jnp.int32(2**30))
    )
    return first, last


def pair_limits(lengths_ref, query_start, key_start, rows):
    first, last = user_bounds(lengths_ref, query_start)
    live = first <= key_start + rows - 1
    query_rows = jnp.where(live, jnp.minimum(last - query_start, rows), 0)
    key_row = jnp.maximum(first - key_start, 0)
    return query_rows, key_row


def scores(q, g, k, v, mask=None):
    nt = (((1,), (1,)), ((), ()))
    half = lax.dot_general(k, q, nt, preferred_element_type=F32) * (0.5 * q.shape[1] ** -0.5)
    da = lax.dot_general(v, g, nt, preferred_element_type=F32)
    gate = 1.0 + jnp.tanh(half)
    if mask is not None:
        gate = jnp.where(mask, gate, 0.0)
    a = half * gate
    f = (gate + a * (2.0 - gate)) * da
    return a.astype(BF16), f.astype(BF16)


def add_block(qs, ks, q, g, k, a, f, dq_ref, dk_ref, dv_ref):
    dv_ref[ks, :] += jnp.dot(a, g, preferred_element_type=F32)
    dk_ref[ks, :] += jnp.dot(f, q, preferred_element_type=F32)
    dq_ref[qs, :] += lax.dot_general(f, k, (((0,), (0,)), ((), ())), preferred_element_type=F32)


def copy_rows(out_ref, ref, start, count, low, high):
    src, dst = pl.ds(start, count), pl.ds(0, count)
    inside = (low <= 0) & (high >= count)

    @pl.when(inside)
    def _():
        for n in range(2):
            out_ref[n, dst, :] = ref[n, src, :]

    @pl.when(jnp.logical_not(inside))
    def _():
        row = lax.broadcasted_iota(jnp.int32, (count, ref.shape[2]), 0)
        kept = (row >= low) & (row < high)
        for n in range(2):
            out_ref[n, dst, :] = jnp.where(kept, ref[n, src, :], jnp.zeros((), BF16))


def sweep(
    qg_ref, kv_ref, dq_ref, dk_ref, dv_ref, query_rows, key_row, key_blocks, qm_ref, km_ref
):
    block = qg_ref.shape[1]
    strip = block // 2

    def run(queries):
        qs = pl.ds(0, queries)
        copy_rows(qm_ref, qg_ref, 0, queries, 0, query_rows)

        def keys(start, count):
            off = pl.multiple_of(start, strip)
            copy_rows(km_ref, kv_ref, off, count, key_row - off, count)
            q, g = qm_ref[0, qs, :], qm_ref[1, qs, :]
            k, v = km_ref[0, pl.ds(0, count), :], km_ref[1, pl.ds(0, count), :]
            a, f = scores(q, g, k, v)
            add_block(qs, pl.ds(off, count), q, g, k, a, f, dq_ref, dk_ref, dv_ref)

        first = key_row // block
        short = key_row - first * block >= strip

        @pl.when(short)
        def _():
            keys(first * block + strip, strip)

        def key_block(kb, carry):
            keys(kb * block, block)
            return carry

        lax.fori_loop(first + short.astype(jnp.int32), key_blocks, key_block, 0)

    @pl.when((query_rows > 0) & (query_rows <= strip))
    def _():
        run(strip)

    @pl.when(query_rows > strip)
    def _():
        run(block)


def halves(ref):
    half = ref.shape[0] // 2
    return ref.at[pl.ds(0, half)], ref.at[pl.ds(half, half)]


def pack_kernel(q_hbm, g_hbm, k_hbm, v_hbm, qa_ref, qb_ref, kv_ref, sems):
    half = qa_ref.shape[1]
    copies = [
        pltpu.make_async_copy(k_hbm, kv_ref.at[0], sems.at[0]),
        pltpu.make_async_copy(v_hbm, kv_ref.at[1], sems.at[1]),
    ]
    for n, ref in enumerate((qa_ref, qb_ref)):
        for m, hbm in enumerate((q_hbm, g_hbm)):
            part = hbm.at[pl.ds(n * half, half)]
            copies.append(pltpu.make_async_copy(part, ref.at[m], sems.at[2 + 2 * n + m]))
    for copy in copies:
        copy.start()
    for copy in copies:
        copy.wait()


def own_kernel(lengths_ref, qa_ref, qb_ref, kv_ref, dq_ref, dk_ref, dv_ref, *masked):
    block = qa_ref.shape[1]
    strip = block // 2
    start = lax.axis_index("seq") * (2 * block)
    dq_ref[...] = jnp.zeros_like(dq_ref)
    dk_ref[...] = jnp.zeros_like(dk_ref)
    dv_ref[...] = jnp.zeros_like(dv_ref)

    for b, qg_ref in enumerate((qa_ref, qb_ref)):
        query = lax.broadcasted_iota(jnp.int32, (1, block), 1) + start + b * block

        def step(u, carry):
            end, first = carry
            end = end + lengths_ref[u]
            return end, jnp.where(end <= query, end, first)

        _, first = lax.fori_loop(
            0, lengths_ref.shape[0], step, (jnp.int32(0), jnp.zeros((1, block), jnp.int32))
        )
        for off in range(0, block, strip):
            ks, qs = pl.ds(b * block + off, strip), pl.ds(b * block + off, block - off)
            key = lax.broadcasted_iota(jnp.int32, (strip, block - off), 0) + start + b * block + off
            mask = (key <= query[:, off:]) & (key >= first[:, off:])
            q, g = qg_ref[0, off:, :], qg_ref[1, off:, :]
            k, v = kv_ref[0, ks, :], kv_ref[1, ks, :]
            a, f = scores(q, g, k, v, mask)
            add_block(qs, ks, q, g, k, a, f, dq_ref, dk_ref, dv_ref)

    query_rows, key_row = pair_limits(lengths_ref, start + block, start, block)
    sweep(qb_ref, kv_ref, halves(dq_ref)[1], dk_ref, dv_ref, query_rows, key_row, 1, *masked)


def next_kernel(
    lengths_ref, qan_ref, kv_ref, dk_in, dv_in, dqn_ref, dk_ref, dv_ref, *masked
):
    rows = kv_ref.shape[1]
    me = lax.axis_index("seq")
    dqn_ref[...] = jnp.zeros_like(dqn_ref)
    query_rows, key_row = pair_limits(lengths_ref, (me + 1) * rows, me * rows, rows)
    sweep(qan_ref, kv_ref, dqn_ref, dk_ref, dv_ref, query_rows, key_row, 2, *masked)


def near_kernel(
    lengths_ref, qa_ref, qb_ref, kvn_ref, dq_in, dq_ref, dkn_ref, dvn_ref, *masked
):
    half, rows = qa_ref.shape[1], kvn_ref.shape[1]
    me = lax.axis_index("seq")
    dkn_ref[...] = jnp.zeros_like(dkn_ref)
    dvn_ref[...] = jnp.zeros_like(dvn_ref)
    query_rows, key_row = pair_limits(lengths_ref, me * rows, (me - 2) * rows, rows)
    for n, (qg_ref, dq) in enumerate(zip((qa_ref, qb_ref), halves(dq_ref))):
        sweep(qg_ref, kvn_ref, dq, dkn_ref, dvn_ref, query_rows - n * half, key_row, 2, *masked)


def rest_kernel(
    lengths_ref, qan_ref, qbn_ref, kv_ref, kvn_ref,
    dq_ref, dqa_in, dk_in, dv_in, dkn_in, dvn_in,
    keep_ref, send_ref, dq_same, dq_cross, dkv_same, dkv_cross,
    dqa_ref, dk_own, dv_own, dk_ref, dv_ref,
    dqb_ref, *masked,
):
    width = dq_ref.shape[1]
    rows = kv_ref.shape[1]
    me = lax.axis_index("seq")
    dqb_ref[...] = jnp.zeros_like(dqb_ref)
    query_rows, key_row = pair_limits(lengths_ref, (me + 1) * rows, me * rows, rows)
    tail_rows = query_rows - rows // 2
    sweep(qbn_ref, kv_ref, dqb_ref, dk_own, dv_own, tail_rows, key_row, 2, *masked)
    query_rows, key_row = pair_limits(lengths_ref, (me + 1) * rows, (me - 2) * rows, rows)
    tail_rows = query_rows - rows // 2
    sweep(qan_ref, kvn_ref, dqa_ref, dk_ref, dv_ref, query_rows, key_row, 2, *masked)
    sweep(qbn_ref, kvn_ref, dqb_ref, dk_ref, dv_ref, tail_rows, key_row, 2, *masked)

    norm = MAXLEN**-0.5
    inner = 0.5 * norm * width**-0.5
    half = dq_same.shape[0]
    block = half // 2
    head = lax.axis_index("head")
    high, low = head // 2, head % 2
    for bit, dq_out, dkv_out in ((high, dq_same, dkv_same), (1 - high, dq_cross, dkv_cross)):
        src = pl.ds(pl.multiple_of(bit * half, half), half)
        dq_out[...] = (jnp.where(bit == 0, dqa_ref[...], dqb_ref[...]) * inner).astype(BF16)
        dkv_out[0] = (dk_ref[src, :] * inner).astype(BF16)
        dkv_out[1] = (dv_ref[src, :] * norm).astype(BF16)
    for bit, out_ref in ((low, keep_ref), (1 - low, send_ref)):
        for top in range(2):
            src = pl.ds(pl.multiple_of((2 * top + bit) * block, block), block)
            dst = pl.ds(top * block, block)
            own = (dq_ref[src, :] * inner, dk_own[src, :] * inner, dv_own[src, :] * norm)
            for c, part in enumerate(own):
                out_ref[c, dst, :] = part.astype(BF16)


def project(grads, weights):
    return lax.dot_general(
        jnp.concatenate(grads, axis=1), jnp.concatenate(weights, axis=1),
        (((1,), (1,)), ((), ())), preferred_element_type=F32,
    )


def local_kernel(keep_ref, got_ref, w_ref, w1_ref, mine_ref, send_ref):
    block = mine_ref.shape[0]
    high = lax.axis_index("head") // 2
    weights = [ref[c] for ref in (w_ref, w1_ref) for c in range(3)]
    for bit, out_ref in ((1 - high, send_ref), (high, mine_ref)):
        src = pl.ds(pl.multiple_of(bit * block, block), block)
        grads = [ref[c, src, :] for ref in (keep_ref, got_ref) for c in range(3)]
        out_ref[...] = project(grads, weights).astype(out_ref.dtype)


def split_kernel(dq_same, dkv_same, dq_cross, dkv_cross, keep_ref, send_ref):
    block = keep_ref.shape[2]
    low = lax.axis_index("head") % 2
    for bit, out_ref in ((1 - low, send_ref), (low, keep_ref)):
        src = pl.ds(pl.multiple_of(bit * block, block), block)
        for n, (dq, dkv) in enumerate(((dq_same, dkv_same), (dq_cross, dkv_cross))):
            out_ref[n, 0] = dq[src, :]
            out_ref[n, 1] = dkv[0, src, :]
            out_ref[n, 2] = dkv[1, src, :]


def returned(half_ref, weights):
    grads = [half_ref[n, c] for n in range(2) for c in range(3)]
    return project(grads, [weight[c] for weight in weights for c in range(3)])


def partial_kernel(keep_ref, mine_ref, w_ref, w2_ref, out_ref):
    out_ref[...] = mine_ref[...] + returned(keep_ref, (w_ref, w2_ref))


def final_kernel(got_ref, partial_ref, arrived_ref, w1_ref, w3_ref, out_ref):
    out_ref[...] = (
        partial_ref[...] + arrived_ref[...].astype(F32) + returned(got_ref, (w1_ref, w3_ref))
    )


def call(body, outs, args, flops, scratch=(), lengths=True, space=VMEM, aliases=()):
    specs = [SMEM if lengths and n == 0 else space for n in range(len(args))]
    moved = sum(math.prod(a.shape) * a.dtype.itemsize for a in (*args, *outs))
    return pl.pallas_call(
        body,
        out_shape=outs,
        in_specs=specs,
        out_specs=tuple(VMEM for _ in outs),
        scratch_shapes=scratch,
        input_output_aliases=dict(aliases),
        compiler_params=pltpu.CompilerParams(vmem_limit_bytes=24 * 2**20),
        cost_estimate=pl.CostEstimate(flops=flops, bytes_accessed=moved, transcendentals=0),
    )(*args)


def shards(queries, keys, values, out_grad, lengths, w_proj):
    rows, width = queries.shape
    model = w_proj.shape[1]
    heads = lax.axis_size("head")
    block = rows // heads
    like = jax.ShapeDtypeStruct
    wide = like((rows, width), F32)
    pair_flops = 10 * rows * rows * width

    half = like((2, rows // 2, width), BF16)
    half_wide = like((rows // 2, width), F32)
    inputs = (queries, out_grad, keys, values)
    qa, qb, kv = call(
        pack_kernel, (half, half, like((2, rows, width), BF16)),
        tuple(pltpu.with_memory_space_constraint(x, pltpu.HBM) for x in inputs), 1000,
        scratch=[pltpu.SemaphoreType.DMA((6,))], lengths=False,
        space=pl.BlockSpec(memory_space=pltpu.HBM),
    )
    kvn = shift(kv, 2)
    qan = shift(qa, -1)
    qbn = shift(qb, -1)
    w2 = shift(w_proj, 0, 2)

    masked = [pltpu.VMEM((2, rows // 2, width), BF16)] * 2
    dq, dk, dv = call(
        own_kernel, (wide, wide, wide), (lengths, qa, qb, kv), pair_flops, scratch=masked
    )
    dqn, dk, dv = call(
        next_kernel, (half_wide, wide, wide), (lengths, qan, kv, dk, dv), pair_flops,
        scratch=masked, aliases=((3, 1), (4, 2)),
    )
    dq, dkn, dvn = call(
        near_kernel, (wide, wide, wide), (lengths, qa, qb, kvn, dq), pair_flops,
        scratch=masked, aliases=((4, 0),),
    )
    keep, send, dq_same, dq_cross, dkv_same, dkv_cross, *_ = call(
        rest_kernel,
        (
            like((3, 2 * block, width), BF16), like((3, 2 * block, width), BF16),
            like((2 * block, width), BF16), like((2 * block, width), BF16),
            like((2, 2 * block, width), BF16), like((2, 2 * block, width), BF16),
            half_wide, wide, wide, wide, wide,
        ),
        (lengths, qan, qbn, kv, kvn, dq, dqn, dk, dv, dkn, dvn), pair_flops,
        scratch=[pltpu.VMEM((rows // 2, width), F32), *masked],
        aliases=((6, 6), (7, 7), (8, 8), (9, 9), (10, 10)),
    )
    w1, w3 = shift(w_proj, 0, 1), shift(w2, 0, 1)
    dkv_cross = shift(dkv_cross, -2, 2)
    dkv_same = shift(dkv_same, -2)
    dq_cross = shift(dq_cross, 1, 2)
    dq_same = shift(dq_same, 1)
    got = shift(send, 0, 1)
    mine, send = call(
        local_kernel, (like((block, model), F32), like((block, model), BF16)),
        (keep, got, w_proj, w1), 12 * block * width * model, lengths=False,
    )
    arrived = shift(send, 0, 2)

    quarter = like((2, 3, block, width), BF16)
    keep, send = call(
        split_kernel, (quarter, quarter), (dq_same, dkv_same, dq_cross, dkv_cross), 1000,
        lengths=False,
    )
    got = shift(send, 0, 1)
    (mine,) = call(
        partial_kernel, (like((block, model), F32),), (keep, mine, w_proj, w2),
        12 * block * width * model, lengths=False,
    )
    (out,) = call(
        final_kernel, (like((block, model), F32),), (got, mine, arrived, w1, w3),
        12 * block * width * model, lengths=False,
    )
    return out


def solution(mesh):
    return jax.shard_map(
        shards,
        mesh=mesh,
        in_specs=(
            P("seq", "head"),
            P("seq", "head"),
            P("seq", "head"),
            P("seq", "head"),
            P(),
            P(None, None, "head"),
        ),
        out_specs=P(("seq", "head"), None),
        check_vma=False,
    )
```

```python
import math

import jax
import jax.numpy as jnp
from jax import lax
from jax.experimental import pallas as pl
from jax.experimental.pallas import tpu as pltpu
from jax.sharding import PartitionSpec as P


MAXLEN = 3072
F32 = jnp.float32
BF16 = jnp.bfloat16
VMEM = pl.BlockSpec(memory_space=pltpu.VMEM)
SMEM = pl.BlockSpec(memory_space=pltpu.SMEM)


def shift(value, by, flip=0):
    tiles, heads = lax.axis_size("seq"), lax.axis_size("head")
    pairs = [
        (t * heads + h, (t + by) * heads + (h ^ flip))
        for t in range(tiles)
        for h in range(heads)
        if 0 <= t + by < tiles
    ]
    return lax.ppermute(value, ("seq", "head"), pairs)


def user_bounds(lengths_ref, position):
    def step(u, carry):
        end, first, last = carry
        end = end + lengths_ref[u]
        past = end <= position
        return (
            end,
            jnp.where(past, end, first),
            jnp.where(past, last, jnp.minimum(last, end)),
        )

    zero = jnp.int32(0)
    _, first, last = lax.fori_loop(
        0, lengths_ref.shape[0], step, (zero, zero, jnp.int32(2**30))
    )
    return first, last


def pair_limits(lengths_ref, query_start, key_start, rows):
    first, last = user_bounds(lengths_ref, query_start)
    live = first <= key_start + rows - 1
    query_rows = jnp.where(live, jnp.minimum(last - query_start, rows), 0)
    key_row = jnp.maximum(first - key_start, 0)
    return query_rows, key_row


def scores(q, g, k, v, mask=None):
    nt = (((1,), (1,)), ((), ()))
    half = lax.dot_general(k, q, nt, preferred_element_type=F32) * (0.5 * q.shape[1] ** -0.5)
    da = lax.dot_general(v, g, nt, preferred_element_type=F32)
    gate = 1.0 + jnp.tanh(half)
    if mask is not None:
        gate = jnp.where(mask, gate, 0.0)
    a = half * gate
    f = (gate + a * (2.0 - gate)) * da
    return a.astype(BF16), f.astype(BF16)


def add_block(qs, ks, q, g, k, a, f, dq_ref, dk_ref, dv_ref):
    dv_ref[ks, :] += jnp.dot(a, g, preferred_element_type=F32)
    dk_ref[ks, :] += jnp.dot(f, q, preferred_element_type=F32)
    dq_ref[qs, :] += lax.dot_general(f, k, (((0,), (0,)), ((), ())), preferred_element_type=F32)


def copy_rows(out_ref, ref, start, count, low, high):
    src, dst = pl.ds(start, count), pl.ds(0, count)
    inside = (low <= 0) & (high >= count)

    @pl.when(inside)
    def _():
        for n in range(2):
            out_ref[n, dst, :] = ref[n, src, :]

    @pl.when(jnp.logical_not(inside))
    def _():
        row = lax.broadcasted_iota(jnp.int32, (count, ref.shape[2]), 0)
        kept = (row >= low) & (row < high)
        for n in range(2):
            out_ref[n, dst, :] = jnp.where(kept, ref[n, src, :], jnp.zeros((), BF16))


def sweep(
    qg_ref, kv_ref, dq_ref, dk_ref, dv_ref, query_rows, key_row, key_blocks, qm_ref, km_ref
):
    block = qg_ref.shape[1]
    strip = block // 2

    def run(queries):
        qs = pl.ds(0, queries)
        copy_rows(qm_ref, qg_ref, 0, queries, 0, query_rows)

        def keys(start, count):
            off = pl.multiple_of(start, strip)
            copy_rows(km_ref, kv_ref, off, count, key_row - off, count)
            q, g = qm_ref[0, qs, :], qm_ref[1, qs, :]
            k, v = km_ref[0, pl.ds(0, count), :], km_ref[1, pl.ds(0, count), :]
            a, f = scores(q, g, k, v)
            add_block(qs, pl.ds(off, count), q, g, k, a, f, dq_ref, dk_ref, dv_ref)

        first = key_row // block
        short = key_row - first * block >= strip

        @pl.when(short)
        def _():
            keys(first * block + strip, strip)

        def key_block(kb, carry):
            keys(kb * block, block)
            return carry

        lax.fori_loop(first + short.astype(jnp.int32), key_blocks, key_block, 0)

    @pl.when((query_rows > 0) & (query_rows <= strip))
    def _():
        run(strip)

    @pl.when(query_rows > strip)
    def _():
        run(block)


def halves(ref):
    half = ref.shape[0] // 2
    return ref.at[pl.ds(0, half)], ref.at[pl.ds(half, half)]


def pack_kernel(q_hbm, g_hbm, k_hbm, v_hbm, qa_ref, qb_ref, kv_ref, sems):
    half = qa_ref.shape[1]
    copies = [
        pltpu.make_async_copy(k_hbm, kv_ref.at[0], sems.at[0]),
        pltpu.make_async_copy(v_hbm, kv_ref.at[1], sems.at[1]),
    ]
    for n, ref in enumerate((qa_ref, qb_ref)):
        for m, hbm in enumerate((q_hbm, g_hbm)):
            part = hbm.at[pl.ds(n * half, half)]
            copies.append(pltpu.make_async_copy(part, ref.at[m], sems.at[2 + 2 * n + m]))
    for copy in copies:
        copy.start()
    for copy in copies:
        copy.wait()


def own_kernel(lengths_ref, qa_ref, qb_ref, kv_ref, dq_ref, dk_ref, dv_ref, *masked):
    block = qa_ref.shape[1]
    strip = block // 2
    start = lax.axis_index("seq") * (2 * block)
    dq_ref[...] = jnp.zeros_like(dq_ref)
    dk_ref[...] = jnp.zeros_like(dk_ref)
    dv_ref[...] = jnp.zeros_like(dv_ref)

    for b, qg_ref in enumerate((qa_ref, qb_ref)):
        query = lax.broadcasted_iota(jnp.int32, (1, block), 1) + start + b * block

        def step(u, carry):
            end, first = carry
            end = end + lengths_ref[u]
            return end, jnp.where(end <= query, end, first)

        _, first = lax.fori_loop(
            0, lengths_ref.shape[0], step, (jnp.int32(0), jnp.zeros((1, block), jnp.int32))
        )
        for off in range(0, block, strip):
            ks, qs = pl.ds(b * block + off, strip), pl.ds(b * block + off, block - off)
            key = lax.broadcasted_iota(jnp.int32, (strip, block - off), 0) + start + b * block + off
            mask = (key <= query[:, off:]) & (key >= first[:, off:])
            q, g = qg_ref[0, off:, :], qg_ref[1, off:, :]
            k, v = kv_ref[0, ks, :], kv_ref[1, ks, :]
            a, f = scores(q, g, k, v, mask)
            add_block(qs, ks, q, g, k, a, f, dq_ref, dk_ref, dv_ref)

    query_rows, key_row = pair_limits(lengths_ref, start + block, start, block)
    sweep(qb_ref, kv_ref, halves(dq_ref)[1], dk_ref, dv_ref, query_rows, key_row, 1, *masked)


def next_kernel(
    lengths_ref, qan_ref, kv_ref, dk_in, dv_in, dqn_ref, dk_ref, dv_ref, *masked
):
    rows = kv_ref.shape[1]
    me = lax.axis_index("seq")
    dqn_ref[...] = jnp.zeros_like(dqn_ref)
    query_rows, key_row = pair_limits(lengths_ref, (me + 1) * rows, me * rows, rows)
    sweep(qan_ref, kv_ref, dqn_ref, dk_ref, dv_ref, query_rows, key_row, 2, *masked)


def near_kernel(
    lengths_ref, qa_ref, qb_ref, kvn_ref, dq_in, dq_ref, dkn_ref, dvn_ref, *masked
):
    half, rows = qa_ref.shape[1], kvn_ref.shape[1]
    me = lax.axis_index("seq")
    dkn_ref[...] = jnp.zeros_like(dkn_ref)
    dvn_ref[...] = jnp.zeros_like(dvn_ref)
    query_rows, key_row = pair_limits(lengths_ref, me * rows, (me - 2) * rows, rows)
    for n, (qg_ref, dq) in enumerate(zip((qa_ref, qb_ref), halves(dq_ref))):
        sweep(qg_ref, kvn_ref, dq, dkn_ref, dvn_ref, query_rows - n * half, key_row, 2, *masked)


def rest_kernel(
    lengths_ref, qan_ref, qbn_ref, kv_ref, kvn_ref,
    dq_ref, dqa_in, dk_in, dv_in, dkn_in, dvn_in,
    keep_ref, send_ref, dq_same, dq_cross, dkv_same, dkv_cross,
    dqa_ref, dk_own, dv_own, dk_ref, dv_ref,
    dqb_ref, *masked,
):
    width = dq_ref.shape[1]
    rows = kv_ref.shape[1]
    me = lax.axis_index("seq")
    dqb_ref[...] = jnp.zeros_like(dqb_ref)
    query_rows, key_row = pair_limits(lengths_ref, (me + 1) * rows, me * rows, rows)
    tail_rows = query_rows - rows // 2
    sweep(qbn_ref, kv_ref, dqb_ref, dk_own, dv_own, tail_rows, key_row, 2, *masked)
    query_rows, key_row = pair_limits(lengths_ref, (me + 1) * rows, (me - 2) * rows, rows)
    tail_rows = query_rows - rows // 2
    sweep(qan_ref, kvn_ref, dqa_ref, dk_ref, dv_ref, query_rows, key_row, 2, *masked)
    sweep(qbn_ref, kvn_ref, dqb_ref, dk_ref, dv_ref, tail_rows, key_row, 2, *masked)

    norm = MAXLEN**-0.5
    inner = 0.5 * norm * width**-0.5
    half = dq_same.shape[0]
    block = half // 2
    head = lax.axis_index("head")
    high, low = head // 2, head % 2
    for bit, dq_out, dkv_out in ((high, dq_same, dkv_same), (1 - high, dq_cross, dkv_cross)):
        src = pl.ds(pl.multiple_of(bit * half, half), half)
        dq_out[...] = (jnp.where(bit == 0, dqa_ref[...], dqb_ref[...]) * inner).astype(BF16)
        dkv_out[0] = (dk_ref[src, :] * inner).astype(BF16)
        dkv_out[1] = (dv_ref[src, :] * norm).astype(BF16)
    for bit, out_ref in ((low, keep_ref), (1 - low, send_ref)):
        for top in range(2):
            src = pl.ds(pl.multiple_of((2 * top + bit) * block, block), block)
            dst = pl.ds(top * block, block)
            own = (dq_ref[src, :] * inner, dk_own[src, :] * inner, dv_own[src, :] * norm)
            for c, part in enumerate(own):
                out_ref[c, dst, :] = part.astype(BF16)


def project(grads, weights):
    return lax.dot_general(
        jnp.concatenate(grads, axis=1), jnp.concatenate(weights, axis=1),
        (((1,), (1,)), ((), ())), preferred_element_type=F32,
    )


def local_kernel(keep_ref, got_ref, w_ref, w1_ref, mine_ref, send_ref):
    block = mine_ref.shape[0]
    high = lax.axis_index("head") // 2
    weights = [ref[c] for ref in (w_ref, w1_ref) for c in range(3)]
    for bit, out_ref in ((1 - high, send_ref), (high, mine_ref)):
        src = pl.ds(pl.multiple_of(bit * block, block), block)
        grads = [ref[c, src, :] for ref in (keep_ref, got_ref) for c in range(3)]
        out_ref[...] = project(grads, weights).astype(out_ref.dtype)


def pair_kernel(same_ref, partner_ref, out_ref):
    out_ref[0] = same_ref[...]
    out_ref[1] = partner_ref[...]


def split_kernel(dq_pair, dkv_same, dkv_cross, keep_ref, send_ref):
    block = keep_ref.shape[2]
    low = lax.axis_index("head") % 2
    for bit, out_ref in ((1 - low, send_ref), (low, keep_ref)):
        src = pl.ds(pl.multiple_of(bit * block, block), block)
        for n, dkv in enumerate((dkv_same, dkv_cross)):
            out_ref[n, 0] = dq_pair[n, src, :]
            out_ref[n, 1] = dkv[0, src, :]
            out_ref[n, 2] = dkv[1, src, :]


def returned(half_ref, weights):
    grads = [half_ref[n, c] for n in range(2) for c in range(3)]
    return project(grads, [weight[c] for weight in weights for c in range(3)])


def partial_kernel(keep_ref, mine_ref, w_ref, w2_ref, out_ref):
    out_ref[...] = mine_ref[...] + returned(keep_ref, (w_ref, w2_ref))


def final_kernel(got_ref, partial_ref, arrived_ref, w1_ref, w3_ref, out_ref):
    out_ref[...] = (
        partial_ref[...] + arrived_ref[...].astype(F32) + returned(got_ref, (w1_ref, w3_ref))
    )


def call(body, outs, args, flops, scratch=(), lengths=True, space=VMEM, aliases=()):
    specs = [SMEM if lengths and n == 0 else space for n in range(len(args))]
    moved = sum(math.prod(a.shape) * a.dtype.itemsize for a in (*args, *outs))
    return pl.pallas_call(
        body,
        out_shape=outs,
        in_specs=specs,
        out_specs=tuple(VMEM for _ in outs),
        scratch_shapes=scratch,
        input_output_aliases=dict(aliases),
        compiler_params=pltpu.CompilerParams(vmem_limit_bytes=24 * 2**20),
        cost_estimate=pl.CostEstimate(flops=flops, bytes_accessed=moved, transcendentals=0),
    )(*args)


def shards(queries, keys, values, out_grad, lengths, w_proj):
    rows, width = queries.shape
    model = w_proj.shape[1]
    heads = lax.axis_size("head")
    block = rows // heads
    like = jax.ShapeDtypeStruct
    wide = like((rows, width), F32)
    pair_flops = 10 * rows * rows * width

    half = like((2, rows // 2, width), BF16)
    half_wide = like((rows // 2, width), F32)
    inputs = (queries, out_grad, keys, values)
    qa, qb, kv = call(
        pack_kernel, (half, half, like((2, rows, width), BF16)),
        tuple(pltpu.with_memory_space_constraint(x, pltpu.HBM) for x in inputs), 1000,
        scratch=[pltpu.SemaphoreType.DMA((6,))], lengths=False,
        space=pl.BlockSpec(memory_space=pltpu.HBM),
    )
    kvn = shift(kv, 2)
    qan = shift(qa, -1)
    qbn = shift(qb, -1)
    w2 = shift(w_proj, 0, 2)

    masked = [pltpu.VMEM((2, rows // 2, width), BF16)] * 2
    dq, dk, dv = call(
        own_kernel, (wide, wide, wide), (lengths, qa, qb, kv), pair_flops, scratch=masked
    )
    dqn, dk, dv = call(
        next_kernel, (half_wide, wide, wide), (lengths, qan, kv, dk, dv), pair_flops,
        scratch=masked, aliases=((3, 1), (4, 2)),
    )
    dq, dkn, dvn = call(
        near_kernel, (wide, wide, wide), (lengths, qa, qb, kvn, dq), pair_flops,
        scratch=masked, aliases=((4, 0),),
    )
    keep, send, dq_same, dq_cross, dkv_same, dkv_cross, *_ = call(
        rest_kernel,
        (
            like((3, 2 * block, width), BF16), like((3, 2 * block, width), BF16),
            like((2 * block, width), BF16), like((2 * block, width), BF16),
            like((2, 2 * block, width), BF16), like((2, 2 * block, width), BF16),
            half_wide, wide, wide, wide, wide,
        ),
        (lengths, qan, qbn, kv, kvn, dq, dqn, dk, dv, dkn, dvn), pair_flops,
        scratch=[pltpu.VMEM((rows // 2, width), F32), *masked],
        aliases=((6, 6), (7, 7), (8, 8), (9, 9), (10, 10)),
    )
    w1, w3 = shift(w_proj, 0, 1), shift(w2, 0, 1)
    partner = shift(dq_cross, 0, 2)
    (dq_pair,) = call(
        pair_kernel, (like((2, rows // 2, width), BF16),), (dq_same, partner), 1000,
        lengths=False,
    )
    dq_pair = shift(dq_pair, 1)
    dkv_cross = shift(dkv_cross, -2, 2)
    dkv_same = shift(dkv_same, -2)
    got = shift(send, 0, 1)
    mine, send = call(
        local_kernel, (like((block, model), F32), like((block, model), BF16)),
        (keep, got, w_proj, w1), 12 * block * width * model, lengths=False,
    )
    arrived = shift(send, 0, 2)

    quarter = like((2, 3, block, width), BF16)
    keep, send = call(
        split_kernel, (quarter, quarter), (dq_pair, dkv_same, dkv_cross), 1000,
        lengths=False,
    )
    got = shift(send, 0, 1)
    (mine,) = call(
        partial_kernel, (like((block, model), F32),), (keep, mine, w_proj, w2),
        12 * block * width * model, lengths=False,
    )
    (out,) = call(
        final_kernel, (like((block, model), F32),), (got, mine, arrived, w1, w3),
        12 * block * width * model, lengths=False,
    )
    return out


def solution(mesh):
    return jax.shard_map(
        shards,
        mesh=mesh,
        in_specs=(
            P("seq", "head"),
            P("seq", "head"),
            P("seq", "head"),
            P("seq", "head"),
            P(),
            P(None, None, "head"),
        ),
        out_specs=P(("seq", "head"), None),
        check_vma=False,
    )
```

```python
import math

import jax
import jax.numpy as jnp
from jax import lax
from jax.experimental import pallas as pl
from jax.experimental.pallas import tpu as pltpu
from jax.sharding import PartitionSpec as P


MAXLEN = 3072
F32 = jnp.float32
BF16 = jnp.bfloat16
VMEM = pl.BlockSpec(memory_space=pltpu.VMEM)
SMEM = pl.BlockSpec(memory_space=pltpu.SMEM)


def shift(value, by, flip=0):
    tiles, heads = lax.axis_size("seq"), lax.axis_size("head")
    pairs = [
        (t * heads + h, (t + by) * heads + (h ^ flip))
        for t in range(tiles)
        for h in range(heads)
        if 0 <= t + by < tiles
    ]
    return lax.ppermute(value, ("seq", "head"), pairs)


def user_bounds(lengths_ref, position):
    def step(u, carry):
        end, first, last = carry
        end = end + lengths_ref[u]
        past = end <= position
        return (
            end,
            jnp.where(past, end, first),
            jnp.where(past, last, jnp.minimum(last, end)),
        )

    zero = jnp.int32(0)
    _, first, last = lax.fori_loop(
        0, lengths_ref.shape[0], step, (zero, zero, jnp.int32(2**30))
    )
    return first, last


def pair_limits(lengths_ref, query_start, key_start, rows):
    first, last = user_bounds(lengths_ref, query_start)
    live = first <= key_start + rows - 1
    query_rows = jnp.where(live, jnp.minimum(last - query_start, rows), 0)
    key_row = jnp.maximum(first - key_start, 0)
    return query_rows, key_row


def scores(q, g, k, v, mask=None):
    nt = (((1,), (1,)), ((), ()))
    half = lax.dot_general(k, q, nt, preferred_element_type=F32) * (0.5 * q.shape[1] ** -0.5)
    da = lax.dot_general(v, g, nt, preferred_element_type=F32)
    gate = 1.0 + jnp.tanh(half)
    if mask is not None:
        gate = jnp.where(mask, gate, 0.0)
    a = half * gate
    f = (gate + a * (2.0 - gate)) * da
    return a.astype(BF16), f.astype(BF16)


def add_block(qs, ks, q, g, k, a, f, dq_ref, dk_ref, dv_ref):
    dv_ref[ks, :] += jnp.dot(a, g, preferred_element_type=F32)
    dk_ref[ks, :] += jnp.dot(f, q, preferred_element_type=F32)
    dq_ref[qs, :] += lax.dot_general(f, k, (((0,), (0,)), ((), ())), preferred_element_type=F32)


def copy_rows(out_ref, ref, start, count, low, high):
    src, dst = pl.ds(start, count), pl.ds(0, count)
    inside = (low <= 0) & (high >= count)

    @pl.when(inside)
    def _():
        for n in range(2):
            out_ref[n, dst, :] = ref[n, src, :]

    @pl.when(jnp.logical_not(inside))
    def _():
        row = lax.broadcasted_iota(jnp.int32, (count, ref.shape[2]), 0)
        kept = (row >= low) & (row < high)
        for n in range(2):
            out_ref[n, dst, :] = jnp.where(kept, ref[n, src, :], jnp.zeros((), BF16))


def sweep(
    qg_ref, kv_ref, dq_ref, dk_ref, dv_ref, query_rows, key_row, key_blocks, qm_ref, km_ref
):
    block = qg_ref.shape[1]
    strip = block // 2

    def run(queries):
        qs = pl.ds(0, queries)
        copy_rows(qm_ref, qg_ref, 0, queries, 0, query_rows)

        def keys(start, count):
            off = pl.multiple_of(start, strip)
            copy_rows(km_ref, kv_ref, off, count, key_row - off, count)
            q, g = qm_ref[0, qs, :], qm_ref[1, qs, :]
            k, v = km_ref[0, pl.ds(0, count), :], km_ref[1, pl.ds(0, count), :]
            a, f = scores(q, g, k, v)
            add_block(qs, pl.ds(off, count), q, g, k, a, f, dq_ref, dk_ref, dv_ref)

        first = key_row // block
        short = key_row - first * block >= strip

        @pl.when(short)
        def _():
            keys(first * block + strip, strip)

        def key_block(kb, carry):
            keys(kb * block, block)
            return carry

        lax.fori_loop(first + short.astype(jnp.int32), key_blocks, key_block, 0)

    @pl.when((query_rows > 0) & (query_rows <= strip))
    def _():
        run(strip)

    @pl.when(query_rows > strip)
    def _():
        run(block)


def halves(ref):
    half = ref.shape[0] // 2
    return ref.at[pl.ds(0, half)], ref.at[pl.ds(half, half)]


def pack_kernel(q_hbm, g_hbm, k_hbm, v_hbm, qa_ref, qb_ref, kv_ref, sems):
    half = qa_ref.shape[1]
    copies = [
        pltpu.make_async_copy(k_hbm, kv_ref.at[0], sems.at[0]),
        pltpu.make_async_copy(v_hbm, kv_ref.at[1], sems.at[1]),
    ]
    for n, ref in enumerate((qa_ref, qb_ref)):
        for m, hbm in enumerate((q_hbm, g_hbm)):
            part = hbm.at[pl.ds(n * half, half)]
            copies.append(pltpu.make_async_copy(part, ref.at[m], sems.at[2 + 2 * n + m]))
    for copy in copies:
        copy.start()
    for copy in copies:
        copy.wait()


def own_kernel(lengths_ref, qa_ref, qb_ref, kv_ref, dq_ref, dk_ref, dv_ref, *masked):
    block = qa_ref.shape[1]
    strip = block // 2
    start = lax.axis_index("seq") * (2 * block)
    dq_ref[...] = jnp.zeros_like(dq_ref)
    dk_ref[...] = jnp.zeros_like(dk_ref)
    dv_ref[...] = jnp.zeros_like(dv_ref)

    for b, qg_ref in enumerate((qa_ref, qb_ref)):
        query = lax.broadcasted_iota(jnp.int32, (1, block), 1) + start + b * block

        def step(u, carry):
            end, first = carry
            end = end + lengths_ref[u]
            return end, jnp.where(end <= query, end, first)

        _, first = lax.fori_loop(
            0, lengths_ref.shape[0], step, (jnp.int32(0), jnp.zeros((1, block), jnp.int32))
        )
        for off in range(0, block, strip):
            ks, qs = pl.ds(b * block + off, strip), pl.ds(b * block + off, block - off)
            key = lax.broadcasted_iota(jnp.int32, (strip, block - off), 0) + start + b * block + off
            mask = (key <= query[:, off:]) & (key >= first[:, off:])
            q, g = qg_ref[0, off:, :], qg_ref[1, off:, :]
            k, v = kv_ref[0, ks, :], kv_ref[1, ks, :]
            a, f = scores(q, g, k, v, mask)
            add_block(qs, ks, q, g, k, a, f, dq_ref, dk_ref, dv_ref)

    query_rows, key_row = pair_limits(lengths_ref, start + block, start, block)
    sweep(qb_ref, kv_ref, halves(dq_ref)[1], dk_ref, dv_ref, query_rows, key_row, 1, *masked)


def next_kernel(
    lengths_ref, qan_ref, kv_ref, dk_in, dv_in, dqn_ref, dk_ref, dv_ref, *masked
):
    rows = kv_ref.shape[1]
    me = lax.axis_index("seq")
    dqn_ref[...] = jnp.zeros_like(dqn_ref)
    query_rows, key_row = pair_limits(lengths_ref, (me + 1) * rows, me * rows, rows)
    sweep(qan_ref, kv_ref, dqn_ref, dk_ref, dv_ref, query_rows, key_row, 2, *masked)


def near_kernel(
    lengths_ref, qa_ref, qb_ref, qan_ref, kvn_ref, dq_in, dqa_in,
    dq_ref, dqa_ref, dkn_ref, dvn_ref, *masked,
):
    half, rows = qa_ref.shape[1], kvn_ref.shape[1]
    me = lax.axis_index("seq")
    dkn_ref[...] = jnp.zeros_like(dkn_ref)
    dvn_ref[...] = jnp.zeros_like(dvn_ref)
    query_rows, key_row = pair_limits(lengths_ref, me * rows, (me - 2) * rows, rows)
    for n, (qg_ref, dq) in enumerate(zip((qa_ref, qb_ref), halves(dq_ref))):
        sweep(qg_ref, kvn_ref, dq, dkn_ref, dvn_ref, query_rows - n * half, key_row, 2, *masked)
    query_rows, key_row = pair_limits(lengths_ref, (me + 1) * rows, (me - 2) * rows, rows)
    sweep(qan_ref, kvn_ref, dqa_ref, dkn_ref, dvn_ref, query_rows, key_row, 2, *masked)


def rest_kernel(
    lengths_ref, qbn_ref, kv_ref, kvn_ref,
    dq_ref, dqa_ref, dk_in, dv_in, dkn_in, dvn_in,
    keep_ref, send_ref, dq_same, dq_cross, dkv_same, dkv_cross,
    dk_own, dv_own, dk_ref, dv_ref,
    dqb_ref, *masked,
):
    width = dq_ref.shape[1]
    rows = kv_ref.shape[1]
    me = lax.axis_index("seq")
    dqb_ref[...] = jnp.zeros_like(dqb_ref)
    query_rows, key_row = pair_limits(lengths_ref, (me + 1) * rows, me * rows, rows)
    tail_rows = query_rows - rows // 2
    sweep(qbn_ref, kv_ref, dqb_ref, dk_own, dv_own, tail_rows, key_row, 2, *masked)
    query_rows, key_row = pair_limits(lengths_ref, (me + 1) * rows, (me - 2) * rows, rows)
    tail_rows = query_rows - rows // 2
    sweep(qbn_ref, kvn_ref, dqb_ref, dk_ref, dv_ref, tail_rows, key_row, 2, *masked)

    norm = MAXLEN**-0.5
    inner = 0.5 * norm * width**-0.5
    half = dq_same.shape[0]
    block = half // 2
    head = lax.axis_index("head")
    high, low = head // 2, head % 2
    for bit, dq_out, dkv_out in ((high, dq_same, dkv_same), (1 - high, dq_cross, dkv_cross)):
        src = pl.ds(pl.multiple_of(bit * half, half), half)
        dq_out[...] = (jnp.where(bit == 0, dqa_ref[...], dqb_ref[...]) * inner).astype(BF16)
        dkv_out[0] = (dk_ref[src, :] * inner).astype(BF16)
        dkv_out[1] = (dv_ref[src, :] * norm).astype(BF16)
    for bit, out_ref in ((low, keep_ref), (1 - low, send_ref)):
        for top in range(2):
            src = pl.ds(pl.multiple_of((2 * top + bit) * block, block), block)
            dst = pl.ds(top * block, block)
            own = (dq_ref[src, :] * inner, dk_own[src, :] * inner, dv_own[src, :] * norm)
            for c, part in enumerate(own):
                out_ref[c, dst, :] = part.astype(BF16)


def project(grads, weights):
    return lax.dot_general(
        jnp.concatenate(grads, axis=1), jnp.concatenate(weights, axis=1),
        (((1,), (1,)), ((), ())), preferred_element_type=F32,
    )


def local_kernel(keep_ref, got_ref, w_ref, w1_ref, mine_ref, send_ref):
    block = mine_ref.shape[0]
    high = lax.axis_index("head") // 2
    weights = [ref[c] for ref in (w_ref, w1_ref) for c in range(3)]
    for bit, out_ref in ((1 - high, send_ref), (high, mine_ref)):
        src = pl.ds(pl.multiple_of(bit * block, block), block)
        grads = [ref[c, src, :] for ref in (keep_ref, got_ref) for c in range(3)]
        out_ref[...] = project(grads, weights).astype(out_ref.dtype)


def pair_kernel(same_ref, partner_ref, out_ref):
    out_ref[0] = same_ref[...]
    out_ref[1] = partner_ref[...]


def split_kernel(dq_pair, dkv_same, dkv_cross, keep_ref, send_ref):
    block = keep_ref.shape[2]
    low = lax.axis_index("head") % 2
    for bit, out_ref in ((1 - low, send_ref), (low, keep_ref)):
        src = pl.ds(pl.multiple_of(bit * block, block), block)
        for n, dkv in enumerate((dkv_same, dkv_cross)):
            out_ref[n, 0] = dq_pair[n, src, :]
            out_ref[n, 1] = dkv[0, src, :]
            out_ref[n, 2] = dkv[1, src, :]


def returned(half_ref, weights):
    grads = [half_ref[n, c] for n in range(2) for c in range(3)]
    return project(grads, [weight[c] for weight in weights for c in range(3)])


def partial_kernel(keep_ref, mine_ref, w_ref, w2_ref, out_ref):
    out_ref[...] = mine_ref[...] + returned(keep_ref, (w_ref, w2_ref))


def final_kernel(got_ref, partial_ref, arrived_ref, w1_ref, w3_ref, out_ref):
    out_ref[...] = (
        partial_ref[...] + arrived_ref[...].astype(F32) + returned(got_ref, (w1_ref, w3_ref))
    )


def call(body, outs, args, flops, scratch=(), lengths=True, space=VMEM, aliases=()):
    specs = [SMEM if lengths and n == 0 else space for n in range(len(args))]
    moved = sum(math.prod(a.shape) * a.dtype.itemsize for a in (*args, *outs))
    return pl.pallas_call(
        body,
        out_shape=outs,
        in_specs=specs,
        out_specs=tuple(VMEM for _ in outs),
        scratch_shapes=scratch,
        input_output_aliases=dict(aliases),
        compiler_params=pltpu.CompilerParams(vmem_limit_bytes=24 * 2**20),
        cost_estimate=pl.CostEstimate(flops=flops, bytes_accessed=moved, transcendentals=0),
    )(*args)


def shards(queries, keys, values, out_grad, lengths, w_proj):
    rows, width = queries.shape
    model = w_proj.shape[1]
    heads = lax.axis_size("head")
    block = rows // heads
    like = jax.ShapeDtypeStruct
    wide = like((rows, width), F32)
    pair_flops = 10 * rows * rows * width

    half = like((2, rows // 2, width), BF16)
    half_wide = like((rows // 2, width), F32)
    inputs = (queries, out_grad, keys, values)
    qa, qb, kv = call(
        pack_kernel, (half, half, like((2, rows, width), BF16)),
        tuple(pltpu.with_memory_space_constraint(x, pltpu.HBM) for x in inputs), 1000,
        scratch=[pltpu.SemaphoreType.DMA((6,))], lengths=False,
        space=pl.BlockSpec(memory_space=pltpu.HBM),
    )
    kvn = shift(kv, 2)
    qan = shift(qa, -1)
    qbn = shift(qb, -1)
    w2 = shift(w_proj, 0, 2)

    masked = [pltpu.VMEM((2, rows // 2, width), BF16)] * 2
    dq, dk, dv = call(
        own_kernel, (wide, wide, wide), (lengths, qa, qb, kv), pair_flops, scratch=masked
    )
    dqn, dk, dv = call(
        next_kernel, (half_wide, wide, wide), (lengths, qan, kv, dk, dv), pair_flops,
        scratch=masked, aliases=((3, 1), (4, 2)),
    )
    dq, dqn, dkn, dvn = call(
        near_kernel, (wide, half_wide, wide, wide),
        (lengths, qa, qb, qan, kvn, dq, dqn), pair_flops,
        scratch=masked, aliases=((5, 0), (6, 1)),
    )
    keep, send, dq_same, dq_cross, dkv_same, dkv_cross, *_ = call(
        rest_kernel,
        (
            like((3, 2 * block, width), BF16), like((3, 2 * block, width), BF16),
            like((2 * block, width), BF16), like((2 * block, width), BF16),
            like((2, 2 * block, width), BF16), like((2, 2 * block, width), BF16),
            wide, wide, wide, wide,
        ),
        (lengths, qbn, kv, kvn, dq, dqn, dk, dv, dkn, dvn), pair_flops,
        scratch=[pltpu.VMEM((rows // 2, width), F32), *masked],
        aliases=((6, 6), (7, 7), (8, 8), (9, 9)),
    )
    w1, w3 = shift(w_proj, 0, 1), shift(w2, 0, 1)
    partner = shift(dq_cross, 0, 2)
    (dq_pair,) = call(
        pair_kernel, (like((2, rows // 2, width), BF16),), (dq_same, partner), 1000,
        lengths=False,
    )
    dq_pair = shift(dq_pair, 1)
    dkv_cross = shift(dkv_cross, -2, 2)
    dkv_same = shift(dkv_same, -2)
    got = shift(send, 0, 1)
    mine, send = call(
        local_kernel, (like((block, model), F32), like((block, model), BF16)),
        (keep, got, w_proj, w1), 12 * block * width * model, lengths=False,
    )
    arrived = shift(send, 0, 2)

    quarter = like((2, 3, block, width), BF16)
    keep, send = call(
        split_kernel, (quarter, quarter), (dq_pair, dkv_same, dkv_cross), 1000,
        lengths=False,
    )
    got = shift(send, 0, 1)
    (mine,) = call(
        partial_kernel, (like((block, model), F32),), (keep, mine, w_proj, w2),
        12 * block * width * model, lengths=False,
    )
    (out,) = call(
        final_kernel, (like((block, model), F32),), (got, mine, arrived, w1, w3),
        12 * block * width * model, lengths=False,
    )
    return out


def solution(mesh):
    return jax.shard_map(
        shards,
        mesh=mesh,
        in_specs=(
            P("seq", "head"),
            P("seq", "head"),
            P("seq", "head"),
            P("seq", "head"),
            P(),
            P(None, None, "head"),
        ),
        out_specs=P(("seq", "head"), None),
        check_vma=False,
    )
```
